128 devices in a mesh: req: 16 (over z, x), head: 8 (over y, core).
Axes of the slice: x: 4, y: 4, z: 4, core: 2. Of those that a mesh axis runs over, the one named last changes fastest.
Arguments:
- residual: bfloat16 [256, 4096], P(None, 'req'), may hold values from -80 to 80
- lengths: int32 [256], P('req'), may hold values from 0 to 32768, as said below
- ssm_state: float32 [256, 128, 64, 128], P('req', 'head'), may hold values from -6 to 6
- tail_mix: float32 [256, 3, 8192], P('req', None, 'head'), may hold values from -6 to 6
- tail_group: float32 [256, 3, 2, 1024], P('req', None, None, 'head'), may hold values from -6 to 6
- norm_first: float32 [4096], P('req'), may hold values from 0.1 to 1.9
- mix_weight: bfloat16 [4096, 2, 8192], P('req', None, 'head'), may hold values from -0.09375 to 0.09375
- group_weight: bfloat16 [4096, 2, 1024], P('req', None, 'head'), may hold values from -0.09375 to 0.09375
- step_weight: bfloat16 [4096, 128], P('req', 'head'), may hold values from -0.09375 to 0.09375
- conv_mix: float32 [4, 8192], P(None, 'head'), may hold values from -3 to 3
- conv_group: float32 [4, 2, 1024], P(None, None, 'head'), may hold values from -3 to 3
- bias_mix: float32 [8192], P('head'), may hold values from -3 to 3
- bias_group: float32 [2, 1024], P(None, 'head'), may hold values from -3 to 3
- step_bias: float32 [128], P('head'), may hold values from -2 to 1
- decay_log: float32 [128], P('head'), may hold values from -1 to 2
- skip_gain: float32 [128], P('head'), may hold values from 0.5 to 2
- gate_gain: float32 [8192], P('head'), may hold values from 0.1 to 1.9
- out_weight: bfloat16 [8192, 4096], P('head', 'req'), may hold values from -0.0625 to 0.0625
- norm_second: float32 [4096], P('req'), may hold values from 0.1 to 1.9
- up_weight: bfloat16 [4096, 21504], P('req', 'head'), may hold values from -0.09375 to 0.09375
- down_weight: bfloat16 [21504, 4096], P('head', 'req'), may hold values from -0.0390625 to 0.0390625
Outputs:
- residual_out: bfloat16 [256, 4096], P(None, 'req')
- state_out: float32 [256, 128, 64, 128], P('req', 'head')
- tail_mix_out: float32 [256, 3, 8192], P('req', None, 'head')
- tail_group_out: float32 [256, 3, 2, 1024], P('req', None, None, 'head')
The draws below stay inside these ranges and needn't reach their ends.
Inputs may be any that keep to these rules, and one draw needn't show every extreme that they name: `lengths`: 0 marks a fresh request.
All inputs are finite; a program needn't handle non-finite values.
Results may differ from the reference program's by a relative error of at most 0.0056.
Values may be sent and summed in bfloat16 or wider, within the bound.
No kernel may reach another device: no remote copies, remote signals or barrier semaphores. Data moves between devices by JAX's collectives and lax.ppermute only.
A program may use at most 128 MiB of HBM per device.

```python
import jax
import jax.numpy as jnp
from jax import lax

D = 4096
FF = 21504
HEADS = 128
HEAD_DIM = 64
GROUPS = 8
STATE = 128
CONV = 4
MAX_LEN = 32768
R = 256


def draw_lengths(key, part):
    subkeys = jax.random.split(key, 4)
    categories = jax.random.randint(subkeys[0], (R,), 0, 8)
    long_lengths = jax.random.randint(subkeys[1], (R,), 3, MAX_LEN + 1)
    drawn = jnp.where(categories == 0, 0, jnp.where(categories == 1, 1, jnp.where(categories == 2, 2, long_lengths)))
    first_index = jax.random.randint(subkeys[2], (), 0, R)
    second_index = (first_index + jax.random.randint(subkeys[3], (), 1, R)) % R
    positions = jnp.arange(R)
    drawn = jnp.where(positions == first_index, MAX_LEN, drawn)
    drawn = jnp.where(positions == second_index, 0, drawn)
    return drawn.astype(jnp.int32)


def draw_residual(key, part):
    noise_key, row_key = jax.random.split(key)
    column = jnp.arange(D).astype(jnp.float32) / (D - 1)
    row_scale = jnp.power(10.0, jax.random.uniform(row_key, (R, 1), jnp.float32, -0.5, 0.5))
    noise = jnp.clip(jax.random.normal(noise_key, (R, D), jnp.float32), -6.0, 6.0)
    column_scale = 0.4 * jnp.power(10.0, column)
    return (noise * row_scale * column_scale[None, :]).astype(jnp.bfloat16)


def levels(stream_key, dims, cuts, low, top_value):
    def one(dim, parts):
        steps = jax.random.uniform(jax.random.fold_in(jax.random.fold_in(stream_key, 6), dim), (parts,), jnp.float32, low / len(cuts), top_value / len(cuts))
        return jnp.repeat(jnp.exp(steps), dims[dim] // parts).reshape((-1,) + (1,) * (len(dims) - dim - 1))

    level = one(*cuts[0])
    for cut in cuts[1:]:
        level = level * one(*cut)
    return level


def bell_draw(key, dims, spread, reach, pieces=(), dtype=jnp.bfloat16):
    values = jax.random.normal(key, dims, jnp.float32) * spread
    if len(pieces) > 0:
        values = levels(key, dims, pieces, -0.22, 0.18) * values
    return jnp.clip(values, min=-reach, max=reach).astype(dtype)


def setup_inputs(seed: int = 0) -> dict:
    streams_of = jax.random.split(jax.random.key(seed), 22)
    residual = draw_residual(jax.random.fold_in(streams_of[21], 71), 0)
    lengths = draw_lengths(jax.random.fold_in(streams_of[21], 71), 0)
    ssm_state = bell_draw(streams_of[2], (R, HEADS, HEAD_DIM, STATE), 1.0, 6.0, ((0, 16), (1, 8)), jnp.float32)
    tail_mix = bell_draw(streams_of[3], (R, CONV - 1, HEADS * HEAD_DIM), 1.0, 6.0, ((0, 16), (2, 8)), jnp.float32)
    tail_group = bell_draw(streams_of[4], (R, CONV - 1, 2, GROUPS * STATE), 1.0, 6.0, ((0, 16), (3, 8)), jnp.float32)
    norm_first = jnp.clip(1.0 + 0.18 * jax.random.normal(streams_of[5], (D,), jnp.float32), 0.1, 1.9)
    mix_weight = bell_draw(streams_of[6], (D, 2, HEADS * HEAD_DIM), D ** -0.5, 0.09375, ((0, 16), (2, 8)))
    group_weight = bell_draw(streams_of[7], (D, 2, GROUPS * STATE), D ** -0.5, 0.09375, ((0, 16), (2, 8)))
    step_weight = bell_draw(streams_of[8], (D, HEADS), D ** -0.5, 0.09375, ((0, 16), (1, 8)))
    conv_mix = bell_draw(streams_of[9], (CONV, HEADS * HEAD_DIM), CONV ** -0.5, 3.0, ((1, 8),), jnp.float32)
    conv_group = bell_draw(streams_of[10], (CONV, 2, GROUPS * STATE), CONV ** -0.5, 3.0, ((2, 8),), jnp.float32)
    bias_mix = bell_draw(streams_of[11], (HEADS * HEAD_DIM,), 0.5, 3.0, ((0, 8),), jnp.float32)
    bias_group = bell_draw(streams_of[12], (2, GROUPS * STATE), 0.5, 3.0, ((1, 8),), jnp.float32)
    step_bias = jnp.clip(-2.0 + 3.0 * jax.random.uniform(streams_of[13], (HEADS,), jnp.float32) ** levels(streams_of[13], (HEADS,), ((0, 8),), -0.2, 0.2), -2.0, 1.0)
    decay_log = jnp.clip(-1.0 + 3.0 * jax.random.uniform(streams_of[14], (HEADS,), jnp.float32) ** levels(streams_of[14], (HEADS,), ((0, 8),), -0.2, 0.2), -1.0, 2.0)
    skip_gain = jnp.clip(0.5 + 1.5 * jax.random.uniform(streams_of[15], (HEADS,), jnp.float32) ** levels(streams_of[15], (HEADS,), ((0, 8),), -0.2, 0.2), 0.5, 2.0)
    gate_gain = jnp.clip(1.0 + 0.18 * jax.random.normal(streams_of[16], (HEADS * HEAD_DIM,), jnp.float32), 0.1, 1.9)
    out_weight = bell_draw(streams_of[17], (HEADS * HEAD_DIM, D), (HEADS * HEAD_DIM) ** -0.5, 0.0625, ((0, 8), (1, 16)))
    norm_second = jnp.clip(1.0 + 0.18 * jax.random.normal(streams_of[18], (D,), jnp.float32), 0.1, 1.9)
    up_weight = bell_draw(streams_of[19], (D, FF), D ** -0.5, 0.09375, ((0, 16), (1, 8)))
    down_weight = bell_draw(streams_of[20], (FF, D), FF ** -0.5, 0.0390625, ((0, 8), (1, 16)))
    return dict(residual=residual, lengths=lengths, ssm_state=ssm_state, tail_mix=tail_mix, tail_group=tail_group, norm_first=norm_first, mix_weight=mix_weight, group_weight=group_weight, step_weight=step_weight, conv_mix=conv_mix, conv_group=conv_group, bias_mix=bias_mix, bias_group=bias_group, step_bias=step_bias, decay_log=decay_log, skip_gain=skip_gain, gate_gain=gate_gain, out_weight=out_weight, norm_second=norm_second, up_weight=up_weight, down_weight=down_weight)


eps = 1e-05

def row_inverse(values):
    wide = values.astype(jnp.float32)
    return lax.rsqrt(lax.optimization_barrier(jnp.mean(wide * wide, axis=1, keepdims=True)) + eps)

def reference(residual, lengths, ssm_state, tail_mix, tail_group, norm_first, mix_weight, group_weight, step_weight, conv_mix, conv_group, bias_mix, bias_group, step_bias, decay_log, skip_gain, gate_gain, out_weight, norm_second, up_weight, down_weight):
    inverse_one = row_inverse(residual)
    scaled = (residual.astype(jnp.float32) * norm_first).astype(jnp.bfloat16)
    gate_z = jnp.dot(scaled, mix_weight[:, 0], preferred_element_type=jnp.float32) * inverse_one
    mix_in = jnp.dot(scaled, mix_weight[:, 1], preferred_element_type=jnp.float32) * inverse_one
    group_in = jnp.stack([jnp.dot(scaled, group_weight[:, 0], preferred_element_type=jnp.float32) * inverse_one, jnp.dot(scaled, group_weight[:, 1], preferred_element_type=jnp.float32) * inverse_one], axis=1)
    step_raw = jnp.dot(scaled, step_weight, preferred_element_type=jnp.float32) * inverse_one
    valid = jnp.minimum(lengths, CONV - 1).astype(jnp.int32)
    slots = jnp.arange(CONV - 1).astype(jnp.int32)
    keep = (slots[None, :] >= (CONV - 1 - valid)[:, None]).astype(jnp.float32)
    window_mix = jnp.concatenate([tail_mix * keep[:, :, None], mix_in[:, None, :]], axis=1)
    window_group = jnp.concatenate([tail_group * keep[:, :, None, None], group_in[:, None]], axis=1)
    conv_x = jax.nn.silu(lax.optimization_barrier(jnp.sum(window_mix * conv_mix[None], axis=1)) + bias_mix)
    conv_bc = jax.nn.silu(lax.optimization_barrier(jnp.sum(window_group * conv_group[None], axis=1)) + bias_group)
    step_size = jax.nn.softplus(step_raw + step_bias)
    alive = (lengths > 0).astype(jnp.float32)
    decay = jnp.exp(-step_size * jnp.exp(decay_log)) * alive[:, None]
    per_group = HEADS // GROUPS
    state_parts = []
    output_parts = []
    for group_id in range(GROUPS):
        first_head = group_id * per_group
        prior = ssm_state[:, first_head:first_head + per_group]
        inputs = conv_x[:, first_head * HEAD_DIM:(first_head + per_group) * HEAD_DIM].reshape(R, per_group, HEAD_DIM)
        b_vector = conv_bc[:, 0, group_id * STATE:(group_id + 1) * STATE]
        c_vector = conv_bc[:, 1, group_id * STATE:(group_id + 1) * STATE]
        rate = decay[:, first_head:first_head + per_group]
        stride = step_size[:, first_head:first_head + per_group]
        updated = rate[:, :, None, None] * prior + (stride[:, :, None] * inputs)[..., None] * b_vector[:, None, None, :]
        readout = jnp.einsum('repn,rn->rep', updated, c_vector, precision=lax.Precision.HIGHEST)
        readout = readout + skip_gain[first_head:first_head + per_group][None, :, None] * inputs
        state_parts.append(updated)
        output_parts.append(readout.reshape(R, per_group * HEAD_DIM))
    state_out = jnp.concatenate(state_parts, axis=1)
    mixed = jnp.concatenate(output_parts, axis=1)
    gated = mixed * jax.nn.silu(gate_z)
    grouped = gated.reshape(R, GROUPS, -1)
    inverse = lax.rsqrt(lax.optimization_barrier(jnp.mean(grouped * grouped, axis=2, keepdims=True)) + eps)
    normed_y = ((grouped * inverse).reshape(R, HEADS * HEAD_DIM) * gate_gain).astype(jnp.bfloat16)
    mixer = jnp.dot(normed_y, out_weight, preferred_element_type=jnp.float32)
    middle = (residual.astype(jnp.float32) + mixer).astype(jnp.bfloat16)
    inverse_two = row_inverse(middle)
    scaled_two = (middle.astype(jnp.float32) * norm_second).astype(jnp.bfloat16)
    activation = jnp.dot(scaled_two, up_weight, preferred_element_type=jnp.float32) * inverse_two
    hidden = jnp.square(jax.nn.relu(activation)).astype(jnp.bfloat16)
    projected = jnp.dot(hidden, down_weight, preferred_element_type=jnp.float32)
    residual_out = (middle.astype(jnp.float32) + projected).astype(jnp.bfloat16)
    return (residual_out, state_out, window_mix[:, 1:], window_group[:, 1:])
```

```python
import jax
import jax.numpy as jnp
from jax import lax
from jax.experimental import pallas as pl
from jax.experimental.pallas import tpu as pltpu
from jax.sharding import Mesh
from jax.sharding import PartitionSpec as P

REQ = ("z", "x")
HEAD = ("y", "c")
LANES = 128
f32 = jnp.float32
bf16 = jnp.bfloat16

eps = 1e-05


def three_parts(total):
    high = total.astype(bf16)
    rest = total - high.astype(f32)
    middle = rest.astype(bf16)
    low = (rest - middle.astype(f32)).astype(bf16)
    return high, middle, low


def silu(v):
    return v / (1.0 + jnp.exp(-v))


def norm_columns(wide, width):
    total = jnp.sum(wide * wide, axis=1, keepdims=True)
    high, middle, low = three_parts(total)
    lane = lax.broadcasted_iota(jnp.int32, (wide.shape[0], LANES), 1)
    zero = jnp.zeros((wide.shape[0], LANES), f32)
    out = jnp.where(lane == width, high.astype(f32), zero)
    out = jnp.where(lane == width + 1, middle.astype(f32), out)
    return jnp.where(lane == width + 2, low.astype(f32), out)


def input_kernel(residual_ref, norm_ref, mix_ref, group_ref, step_ref, out_ref):
    wide = residual_ref[...].astype(f32)
    scaled = (wide * norm_ref[...]).astype(bf16)
    mix = mix_ref.shape[1]
    group = group_ref.shape[1]
    steps = step_ref.shape[0]
    out_ref[:, :mix] = jnp.dot(scaled, mix_ref[...], preferred_element_type=f32).astype(bf16)
    out_ref[:, mix : mix + group] = jnp.dot(scaled, group_ref[...], preferred_element_type=f32).astype(bf16)
    step = lax.dot_general(scaled, step_ref[...], (((1,), (1,)), ((), ())), preferred_element_type=f32)
    tail = norm_columns(wide, steps)
    out_ref[:, mix + group :] = tail.astype(bf16)
    out_ref[:, mix + group : mix + group + steps] = step.astype(bf16)


def input_projection(residual, norm, mix, group, step_t):
    rows = residual.shape[0]
    width = mix.shape[1] + group.shape[1] + LANES
    return pl.pallas_call(
        input_kernel,
        out_shape=jax.ShapeDtypeStruct((rows, width), bf16),
        name="input_projection",
    )(residual, norm, mix, group, step_t)


def make_state_kernel(per_step, width_all, dims):
    pieces, rows, heads, head_dim, state, mix, taps = dims
    steps = rows // per_step

    def kernel(
        arrived_ref, lengths_ref, tail_mix_ref, tail_group_ref, conv_mix_ref, conv_group_ref,
        bias_mix_ref, bias_group_ref, step_bias_ref, decay_log_ref, skip_ref, gain_ref, state_ref,
        y_ref, tail_mix_out_ref, tail_group_out_ref, state_out_ref,
        u_ref, decay_ref, decay_wide_ref, b_ref, c_ref, x_ref, gate_ref, out_acc,
    ):
        i = pl.program_id(0)

        def expand(v):
            row = lax.broadcasted_iota(jnp.int32, (heads, mix), 0)
            col = lax.broadcasted_iota(jnp.int32, (heads, mix), 1)
            spread = (col // head_dim == row).astype(f32)
            return jnp.dot(v, spread, precision=lax.Precision.HIGHEST, preferred_element_type=f32)

        @pl.when(i == 0)
        def _():
            def total(lo, hi):
                acc = arrived_ref[0, :, lo:hi].astype(f32)
                for j in range(1, pieces):
                    acc = acc + arrived_ref[j, :, lo:hi].astype(f32)
                return acc

            base = 2 * mix
            last = total(base + 2 * state, base + 2 * state + LANES)
            squares = last[:, heads : heads + 1] + last[:, heads + 1 : heads + 2] + last[:, heads + 2 : heads + 3]
            inverse = lax.rsqrt(squares / width_all + eps)
            gate_ref[...] = total(0, mix) * inverse
            mix_in = total(mix, base) * inverse
            group_in = [total(base + g * state, base + (g + 1) * state) * inverse for g in range(2)]
            step_raw = last[:, :heads] * inverse
            lengths = lengths_ref[...]
            valid = jnp.minimum(lengths, taps - 1)
            conv = mix_in * conv_mix_ref[taps - 1 : taps, :]
            for j in range(taps - 1):
                keep = (valid >= taps - 1 - j).astype(f32)
                w = tail_mix_ref[j] * keep
                if j > 0:
                    tail_mix_out_ref[j - 1] = w
                conv = conv + w * conv_mix_ref[j : j + 1, :]
            tail_mix_out_ref[taps - 2] = mix_in
            x = silu(conv + bias_mix_ref[...])
            x_ref[...] = x
            for g, dest in ((0, b_ref), (1, c_ref)):
                conv = group_in[g] * conv_group_ref[taps - 1, g : g + 1, :]
                for j in range(taps - 1):
                    keep = (valid >= taps - 1 - j).astype(f32)
                    w = tail_group_ref[:, j, g, :] * keep
                    if j > 0:
                        tail_group_out_ref[:, j - 1, g, :] = w
                    conv = conv + w * conv_group_ref[j, g : g + 1, :]
                tail_group_out_ref[:, taps - 2, g, :] = group_in[g]
                dest[...] = silu(conv + bias_group_ref[g : g + 1, :])
            v = step_raw + step_bias_ref[...]
            step_size = jnp.maximum(v, 0.0) + jnp.log1p(jnp.exp(-jnp.abs(v)))
            alive = (lengths > 0).astype(f32)
            decay = jnp.exp(-step_size * jnp.exp(decay_log_ref[...])) * alive
            decay_wide = expand(decay)
            decay_wide_ref[...] = decay_wide
            decay_ref[...] = jnp.concatenate([decay, jnp.zeros((rows, LANES - heads), f32)], axis=1)
            u = expand(step_size) * x
            for t in range(mix // LANES):
                u_ref[t] = u[:, t * LANES : (t + 1) * LANES]
            out_acc[...] = jnp.zeros_like(out_acc)

        lane = lax.broadcasted_iota(jnp.int32, (state, LANES), 1)
        for k in range(per_step):
            r = i * per_step + k
            b_row = b_ref[pl.ds(r, 1), :]
            c_row = c_ref[pl.ds(r, 1), :]
            c_col = jnp.transpose(jnp.broadcast_to(c_row, (LANES, state)))
            c_high = c_col.astype(bf16)
            c_low = (c_col - c_high.astype(f32)).astype(bf16)
            rhs = jnp.where(lane == r, c_high.astype(f32), 0.0) + jnp.where(lane == r + rows, c_low.astype(f32), 0.0)
            rhs = rhs.astype(bf16)
            d_row = jnp.transpose(jnp.broadcast_to(decay_ref[pl.ds(r, 1), :], (LANES, LANES)))
            for h in range(heads):
                at = h * head_dim
                if at % LANES == 0:
                    u_row = u_ref[at // LANES, pl.ds(r, 1), :]
                    u_col = jnp.transpose(jnp.broadcast_to(u_row, (LANES, LANES)))
                u_h = u_col[at % LANES : at % LANES + head_dim, :]
                s = state_ref[k, h]
                state_out_ref[k, h] = s * d_row[h : h + 1, :] + u_h * b_row
                s_high = s.astype(bf16)
                s_low = (s - s_high.astype(f32)).astype(bf16)
                rows_h = pl.ds(h * head_dim, head_dim)
                out_acc[rows_h, :] += jnp.dot(s_high, rhs, preferred_element_type=f32) + jnp.dot(
                    s_low, rhs, preferred_element_type=f32
                )

        @pl.when(i == steps - 1)
        def _():
            acc = jnp.transpose(out_acc[...])
            read = acc[:rows, :] + acc[rows : 2 * rows, :]
            bc = jnp.sum(b_ref[...] * c_ref[...], axis=1, keepdims=True)
            x = x_ref[...]
            u = jnp.concatenate([u_ref[t] for t in range(mix // LANES)], axis=1)
            mixed = decay_wide_ref[...] * read + u * bc + expand(jnp.broadcast_to(skip_ref[...], (rows, heads))) * x
            gated = mixed * silu(gate_ref[...])
            inverse = lax.rsqrt(jnp.mean(gated * gated, axis=1, keepdims=True) + eps)
            y_ref[...] = (gated * inverse * gain_ref[...]).astype(bf16)

    return kernel


def state_step(arrived, lengths, tail_mix, tail_group, conv_mix, conv_group, bias_mix, bias_group,
               step_bias, decay_log, skip_gain, gate_gain, ssm_state, width_all, per_step=2):
    pieces, rows, width = arrived.shape
    _, heads, head_dim, state = ssm_state.shape
    mix = heads * head_dim
    taps = conv_mix.shape[0]
    args = (
        arrived, lengths[:, None], jnp.transpose(tail_mix, (1, 0, 2)), tail_group, conv_mix, conv_group,
        bias_mix[None], bias_group, step_bias[None], decay_log[None], skip_gain[None], gate_gain[None],
    )

    def whole(shape):
        return pl.BlockSpec(shape, lambda i, n=len(shape): (0,) * n)

    block = pl.BlockSpec((per_step, heads, head_dim, state), lambda i: (i, 0, 0, 0))
    outs = (
        jax.ShapeDtypeStruct((rows, mix), bf16),
        jax.ShapeDtypeStruct((taps - 1, rows, mix), f32),
        jax.ShapeDtypeStruct((rows, taps - 1, 2, state), f32),
        jax.ShapeDtypeStruct(ssm_state.shape, f32),
    )
    y, tail_mix_out, tail_group_out, state_out = pl.pallas_call(
        make_state_kernel(per_step, width_all, (pieces, rows, heads, head_dim, state, mix, taps)),
        grid=(rows // per_step,),
        in_specs=[whole(a.shape) for a in args] + [block],
        out_specs=[whole(o.shape) for o in outs[:3]] + [block],
        out_shape=outs,
        scratch_shapes=[
            pltpu.VMEM((mix // LANES, rows, LANES), f32),
            pltpu.VMEM((rows, LANES), f32),
            pltpu.VMEM((rows, mix), f32),
            pltpu.VMEM((rows, state), f32),
            pltpu.VMEM((rows, state), f32),
            pltpu.VMEM((rows, mix), f32),
            pltpu.VMEM((rows, mix), f32),
            pltpu.VMEM((mix, LANES), f32),
        ],
        name="state_step",
    )(*args, ssm_state)
    return y, jnp.transpose(tail_mix_out, (1, 0, 2)), tail_group_out, state_out


def swap_core(value):
    return lax.ppermute(value, "c", [(0, 1), (1, 0)])


def ring_pairs(value, first):
    n = lax.axis_size("y")
    pairs = []
    for a in range(first, n + first, 2):
        p, q = a % n, (a + 1) % n
        pairs += [(p, q), (q, p)]
    return lax.ppermute(value, "y", pairs)


def head_sum_half(partial):
    half = partial.shape[0] // 2
    core = lax.axis_index("c")
    mine = lax.dynamic_slice_in_dim(partial, core * half, half, 0)
    theirs = lax.dynamic_slice_in_dim(partial, (1 - core) * half, half, 0).astype(bf16)
    total = mine + swap_core(theirs).astype(f32)
    for first in (0, 1):
        sent = total.astype(bf16)
        total = sent.astype(f32) + ring_pairs(sent, first).astype(f32)
    return total, core


def both_halves(half, core):
    other = swap_core(half)
    first = jnp.where(core == 0, half, other)
    second = jnp.where(core == 0, other, half)
    return jnp.concatenate([first, second], axis=0)


def add_over_heads(base, partial):
    total, core = head_sum_half(partial)
    half = total.shape[0]
    mine = lax.dynamic_slice_in_dim(base, core * half, half, 0).astype(f32)
    return both_halves((mine + total).astype(bf16), core)


def exchange(value, axis):
    return lax.all_to_all(value, axis, 0, 0, tiled=True)


def to_everyone(value, axis):
    peers = lax.axis_size(axis)
    copies = jnp.broadcast_to(value[None], (peers, *value.shape))
    return exchange(copies, axis).reshape(peers * value.shape[0], *value.shape[1:])


def on_device(
    residual, lengths, ssm_state, tail_mix, tail_group, norm_first, mix_weight, group_weight, step_weight,
    conv_mix, conv_group, bias_mix, bias_group, step_bias, decay_log, skip_gain, gate_gain, out_weight,
    norm_second, up_weight, down_weight,
):
    peers = lax.axis_size(REQ)
    rows_dev = ssm_state.shape[0]
    rows, width_dev = residual.shape
    width_all = width_dev * peers
    mix_flat = mix_weight.reshape(width_dev, -1)
    group_flat = group_weight.reshape(width_dev, -1)
    pieces = input_projection(residual, norm_first[None], mix_flat, group_flat, step_weight.T)
    arrived = exchange(pieces.reshape(peers, rows_dev, -1), REQ)
    normed_y, tail_mix_out, tail_group_out, state_out = state_step(
        arrived, lengths, tail_mix, tail_group, conv_mix, conv_group, bias_mix, bias_group, step_bias,
        decay_log, skip_gain, gate_gain, ssm_state, width_all,
    )
    every_y = to_everyone(normed_y, REQ)
    middle = add_over_heads(residual, jnp.dot(every_y, out_weight, preferred_element_type=f32))
    wide = middle.astype(f32)
    scaled_two = (wide * norm_second).astype(bf16)
    activation = jnp.dot(scaled_two, up_weight, preferred_element_type=f32).astype(bf16)
    hidden_dev = up_weight.shape[1]
    total = jnp.sum(wide * wide, axis=1, keepdims=True)
    high = lax.reduce_precision(total, 8, 7)
    mid = lax.reduce_precision(total - high, 8, 7)
    low = total - high - mid
    lane = lax.broadcasted_iota(jnp.int32, (rows, LANES), 1)
    columns = jnp.where(lane == 0, high, jnp.where(lane == 1, mid, jnp.where(lane == 2, low, 0.0))).astype(bf16)
    sent = jnp.concatenate([activation, columns], axis=1).reshape(peers, rows_dev, hidden_dev + LANES)
    sums = exchange(sent, REQ).astype(f32).sum(axis=0)
    squares = sums[:, hidden_dev : hidden_dev + 1] + sums[:, hidden_dev + 1 : hidden_dev + 2] + sums[:, hidden_dev + 2 : hidden_dev + 3]
    inverse = lax.rsqrt(squares / width_all + eps)
    hidden = jnp.square(jax.nn.relu(sums[:, :hidden_dev] * inverse)).astype(bf16)
    every_hidden = to_everyone(hidden, REQ)
    residual_out = add_over_heads(middle, jnp.dot(every_hidden, down_weight, preferred_element_type=f32))
    return residual_out, state_out, tail_mix_out, tail_group_out


def solution(mesh):
    devices = mesh.devices
    finer = Mesh(devices.reshape(4, devices.shape[0] // 4, devices.shape[1] // 2, 2), REQ + HEAD)
    placed = (
        P(None, REQ),
        P(REQ),
        P(REQ, HEAD, None, None),
        P(REQ, None, HEAD),
        P(REQ, None, None, HEAD),
        P(REQ),
        P(REQ, None, HEAD),
        P(REQ, None, HEAD),
        P(REQ, HEAD),
        P(None, HEAD),
        P(None, None, HEAD),
        P(HEAD),
        P(None, HEAD),
        P(HEAD),
        P(HEAD),
        P(HEAD),
        P(HEAD),
        P(HEAD, REQ),
        P(REQ),
        P(REQ, HEAD),
        P(HEAD, REQ),
    )
    return jax.shard_map(
        on_device,
        mesh=finer,
        in_specs=placed,
        out_specs=(P(None, REQ), P(REQ, HEAD, None, None), P(REQ, None, HEAD), P(REQ, None, None, HEAD)),
        check_vma=False,
    )
```

```python
import jax
import jax.numpy as jnp
from jax import lax
from jax.experimental import pallas as pl
from jax.experimental.pallas import tpu as pltpu
from jax.sharding import Mesh
from jax.sharding import PartitionSpec as P

REQ = ("z", "x")
HEAD = ("y", "c")
LANES = 128
BATCH = 4
IN_VMEM = pl.BlockSpec(memory_space=pltpu.VMEM)
SMALL = pltpu.CompilerParams(vmem_limit_bytes=16 * 2**20)
f32 = jnp.float32
bf16 = jnp.bfloat16

eps = 1e-05


def three_parts(total):
    high = total.astype(bf16)
    rest = total - high.astype(f32)
    middle = rest.astype(bf16)
    low = (rest - middle.astype(f32)).astype(bf16)
    return high, middle, low


def in_hbm(value):
    return pltpu.with_memory_space_constraint(value, pltpu.HBM)


def silu(v):
    return v / (1.0 + jnp.exp(-v))


def norm_columns(wide, width):
    total = jnp.sum(wide * wide, axis=1, keepdims=True)
    high, middle, low = three_parts(total)
    lane = lax.broadcasted_iota(jnp.int32, (wide.shape[0], LANES), 1)
    zero = jnp.zeros((wide.shape[0], LANES), f32)
    out = jnp.where(lane == width, high.astype(f32), zero)
    out = jnp.where(lane == width + 1, middle.astype(f32), out)
    return jnp.where(lane == width + 2, low.astype(f32), out)


def input_kernel(residual_ref, norm_ref, mix_ref, group_ref, step_ref, out_ref):
    wide = residual_ref[...].astype(f32)
    scaled = (wide * norm_ref[...]).astype(bf16)
    mix = mix_ref.shape[1]
    group = group_ref.shape[1]
    steps = step_ref.shape[0]
    out_ref[:, :mix] = jnp.dot(scaled, mix_ref[...], preferred_element_type=f32).astype(bf16)
    out_ref[:, mix : mix + group] = jnp.dot(scaled, group_ref[...], preferred_element_type=f32).astype(bf16)
    step = lax.dot_general(scaled, step_ref[...], (((1,), (1,)), ((), ())), preferred_element_type=f32)
    tail = norm_columns(wide, steps)
    out_ref[:, mix + group :] = tail.astype(bf16)
    out_ref[:, mix + group : mix + group + steps] = step.astype(bf16)


def input_projection(residual, norm, mix, group, step_t):
    rows = residual.shape[0]
    width = mix.shape[1] + group.shape[1] + LANES
    return pl.pallas_call(
        input_kernel,
        out_shape=jax.ShapeDtypeStruct((rows, width), bf16),
        in_specs=[IN_VMEM] * 5,
        out_specs=IN_VMEM,
        compiler_params=SMALL,
        name="input_projection",
    )(residual, norm, mix, group, step_t)


def expander(heads, mix, head_dim):
    row = lax.broadcasted_iota(jnp.int32, (heads, mix), 0)
    col = lax.broadcasted_iota(jnp.int32, (heads, mix), 1)
    return (col // head_dim == row).astype(f32)


def make_mixer_kernel(width_all, dims):
    pieces, rows, heads, head_dim, state, mix, taps = dims

    def kernel(
        arrived_ref, lengths_ref, tail_mix_ref, tail_group_ref, conv_mix_ref, conv_group_ref,
        bias_mix_ref, bias_group_ref, step_bias_ref, decay_log_ref, skip_ref, gain_ref, state_ref,
        y_ref, tail_mix_out_ref, tail_group_out_ref, u_ref, decay_ref, b_ref,
        c_ref, read_ref, buffer_ref, sems,
    ):
        def fetch(r):
            return pltpu.make_async_copy(state_ref.at[r], buffer_ref.at[r], sems.at[r])

        for r in range(rows):
            fetch(r).start()
        spread = expander(heads, mix, head_dim)

        def expand(v):
            return jnp.dot(v, spread, precision=lax.Precision.HIGHEST, preferred_element_type=f32)

        def total(lo, hi):
            acc = arrived_ref[0, :, lo:hi].astype(f32)
            for j in range(1, pieces):
                acc = acc + arrived_ref[j, :, lo:hi].astype(f32)
            return acc

        base = 2 * mix
        last = total(base + 2 * state, base + 2 * state + LANES)
        squares = last[:, heads : heads + 1] + last[:, heads + 1 : heads + 2] + last[:, heads + 2 : heads + 3]
        inverse = lax.rsqrt(squares / width_all + eps)
        across = jnp.broadcast_to(lengths_ref[...].astype(f32), (rows, rows))
        diagonal = lax.broadcasted_iota(jnp.int32, (rows, rows), 0) == lax.broadcasted_iota(jnp.int32, (rows, rows), 1)
        lengths = jnp.sum(jnp.where(diagonal, across, 0.0), axis=1, keepdims=True)
        valid = jnp.minimum(lengths, taps - 1.0)
        keep = [(valid >= taps - 1.0 - j).astype(f32) for j in range(taps - 1)]
        for g, dest in ((0, b_ref), (1, c_ref)):
            group_in = total(base + g * state, base + (g + 1) * state) * inverse
            conv = group_in * conv_group_ref[taps - 1, g : g + 1, :]
            for j in range(taps - 1):
                w = tail_group_ref[:, j, g, :] * keep[j]
                if j > 0:
                    tail_group_out_ref[:, j - 1, g, :] = w
                conv = conv + w * conv_group_ref[j, g : g + 1, :]
            tail_group_out_ref[:, taps - 2, g, :] = group_in
            dest[...] = silu(conv + bias_group_ref[g : g + 1, :])

        mix_in = total(mix, base) * inverse
        conv = mix_in * conv_mix_ref[taps - 1 : taps, :]
        for j in range(taps - 1):
            w = tail_mix_ref[j] * keep[j]
            if j > 0:
                tail_mix_out_ref[j - 1] = w
            conv = conv + w * conv_mix_ref[j : j + 1, :]
        tail_mix_out_ref[taps - 2] = mix_in
        x = silu(conv + bias_mix_ref[...])
        v = last[:, :heads] * inverse + step_bias_ref[...]
        step_size = jnp.maximum(v, 0.0) + jnp.log1p(jnp.exp(-jnp.abs(v)))
        alive = (lengths > 0.0).astype(f32)
        decay = jnp.exp(-step_size * jnp.exp(decay_log_ref[...])) * alive
        decay_ref[...] = jnp.concatenate([decay, jnp.zeros((rows, LANES - heads), f32)], axis=1)
        u = expand(step_size) * x
        for t in range(mix // LANES):
            u_ref[t] = u[:, t * LANES : (t + 1) * LANES]
        lane = lax.broadcasted_iota(jnp.int32, (head_dim, LANES), 1)
        for first in range(0, rows, BATCH):
            for r in range(first, first + BATCH):
                fetch(r).wait()

            def one_head(h, carry, first=first):
                at = pl.ds(pl.multiple_of(h * head_dim, head_dim), head_dim)
                acc = jnp.zeros((head_dim, LANES), f32) if first == 0 else read_ref[at, :]
                for r in range(first, first + BATCH):
                    part = jnp.sum(buffer_ref[r, h] * c_ref[r : r + 1, :], axis=1, keepdims=True)
                    acc = jnp.where(lane == r, part, acc)
                read_ref[at, :] = acc
                return carry

            lax.fori_loop(0, heads, one_head, 0)

        read = jnp.transpose(read_ref[...])[:rows, :]
        bc = jnp.sum(b_ref[...] * c_ref[...], axis=1, keepdims=True)
        skip = expand(jnp.broadcast_to(skip_ref[...], (rows, heads)))
        mixed = expand(decay) * read + u * bc + skip * x
        gated = mixed * silu(total(0, mix) * inverse)
        inverse_gated = lax.rsqrt(jnp.mean(gated * gated, axis=1, keepdims=True) + eps)
        y = (gated * inverse_gated * gain_ref[...]).astype(bf16)
        for j in range(pieces):
            y_ref[j] = y

    return kernel


def mixer_step(arrived, lengths, tail_mix, tail_group, conv_mix, conv_group, bias_mix, bias_group,
               step_bias, decay_log, skip_gain, gate_gain, ssm_state, width_all):
    pieces, rows, width = arrived.shape
    _, heads, head_dim, state = ssm_state.shape
    mix = heads * head_dim
    taps = conv_mix.shape[0]
    args = (
        arrived, lengths[None], jnp.transpose(tail_mix, (1, 0, 2)), tail_group, conv_mix, conv_group,
        bias_mix[None], bias_group, step_bias[None], decay_log[None], skip_gain[None], gate_gain[None], in_hbm(ssm_state),
    )
    outs = (
        jax.ShapeDtypeStruct((pieces, rows, mix), bf16),
        jax.ShapeDtypeStruct((taps - 1, rows, mix), f32),
        jax.ShapeDtypeStruct((rows, taps - 1, 2, state), f32),
        jax.ShapeDtypeStruct((mix // LANES, rows, LANES), f32),
        jax.ShapeDtypeStruct((rows, LANES), f32),
        jax.ShapeDtypeStruct((rows, state), f32),
    )
    return pl.pallas_call(
        make_mixer_kernel(width_all, (pieces, rows, heads, head_dim, state, mix, taps)),
        in_specs=[IN_VMEM] * (len(args) - 1) + [pl.BlockSpec(memory_space=pl.ANY)],
        out_specs=[IN_VMEM] * len(outs),
        out_shape=outs,
        scratch_shapes=[
            pltpu.VMEM((rows, state), f32),
            pltpu.VMEM((mix, LANES), f32),
            pltpu.VMEM((rows, heads, head_dim, state), f32),
            pltpu.SemaphoreType.DMA((rows,)),
        ],
        compiler_params=SMALL,
        name="mixer_step",
    )(*args)


def make_update_kernel(per_step, heads, head_dim):
    def kernel(u_ref, decay_ref, b_ref, state_ref, out_ref):
        i = pl.program_id(0)
        for k in range(per_step):
            r = i * per_step + k
            b_row = b_ref[pl.ds(r, 1), :]
            d_col = jnp.transpose(jnp.broadcast_to(decay_ref[pl.ds(r, 1), :], (LANES, LANES)))
            for h in range(heads):
                at = h * head_dim
                if at % LANES == 0:
                    u_row = u_ref[at // LANES, pl.ds(r, 1), :]
                    u_col = jnp.transpose(jnp.broadcast_to(u_row, (LANES, LANES)))
                u_h = u_col[at % LANES : at % LANES + head_dim, :]
                out_ref[k, h] = state_ref[k, h] * d_col[h : h + 1, :] + u_h * b_row

    return kernel


def state_update(ssm_state, u, decay, b, per_step=2):
    rows, heads, head_dim, state = ssm_state.shape
    block = pl.BlockSpec((per_step, heads, head_dim, state), lambda i: (i, 0, 0, 0))
    return pl.pallas_call(
        make_update_kernel(per_step, heads, head_dim),
        grid=(rows // per_step,),
        in_specs=[IN_VMEM] * 3 + [block],
        out_specs=block,
        out_shape=jax.ShapeDtypeStruct(ssm_state.shape, f32),
        compiler_params=SMALL,
        name="state_update",
    )(u, decay, b, in_hbm(ssm_state))


def swap_core(value):
    return lax.ppermute(value, "c", [(0, 1), (1, 0)])


def ring_pairs(value, first):
    n = lax.axis_size("y")
    pairs = []
    for a in range(first, n + first, 2):
        p, q = a % n, (a + 1) % n
        pairs += [(p, q), (q, p)]
    return lax.ppermute(value, "y", pairs)


def head_sum_half(partial):
    half = partial.shape[0] // 2
    core = lax.axis_index("c")
    mine = lax.dynamic_slice_in_dim(partial, core * half, half, 0)
    theirs = lax.dynamic_slice_in_dim(partial, (1 - core) * half, half, 0).astype(bf16)
    total = mine + swap_core(theirs).astype(f32)
    for first in (0, 1):
        sent = total.astype(bf16)
        total = sent.astype(f32) + ring_pairs(sent, first).astype(f32)
    return total, core


def both_halves(half, core):
    other = swap_core(half)
    first = jnp.where(core == 0, half, other)
    second = jnp.where(core == 0, other, half)
    return jnp.concatenate([first, second], axis=0)


def add_over_heads(base, partial):
    total, core = head_sum_half(partial)
    half = total.shape[0]
    mine = lax.dynamic_slice_in_dim(base, core * half, half, 0).astype(f32)
    return both_halves((mine + total).astype(bf16), core)


def exchange(value, axis):
    return lax.all_to_all(value, axis, 0, 0, tiled=True)


def to_everyone(value, axis):
    peers = lax.axis_size(axis)
    copies = jnp.broadcast_to(value[None], (peers, *value.shape))
    return exchange(copies, axis).reshape(peers * value.shape[0], *value.shape[1:])


def on_device(
    residual, lengths, ssm_state, tail_mix, tail_group, norm_first, mix_weight, group_weight, step_weight,
    conv_mix, conv_group, bias_mix, bias_group, step_bias, decay_log, skip_gain, gate_gain, out_weight,
    norm_second, up_weight, down_weight,
):
    peers = lax.axis_size(REQ)
    rows_dev = ssm_state.shape[0]
    rows, width_dev = residual.shape
    width_all = width_dev * peers
    mix_flat = mix_weight.reshape(width_dev, -1)
    group_flat = group_weight.reshape(width_dev, -1)
    pieces = input_projection(residual, norm_first[None], mix_flat, group_flat, step_weight.T)
    arrived = exchange(pieces.reshape(peers, rows_dev, -1), REQ)
    copies, tail_mix_out, tail_group_out, u, decay, b = mixer_step(
        arrived, lengths, tail_mix, tail_group, conv_mix, conv_group, bias_mix, bias_group, step_bias,
        decay_log, skip_gain, gate_gain, ssm_state, width_all,
    )
    every_y = exchange(copies, REQ).reshape(rows, -1)
    state_out = state_update(ssm_state, u, decay, b)
    every_y, state_out = lax.optimization_barrier((every_y, state_out))
    middle = add_over_heads(residual, jnp.dot(every_y, out_weight, preferred_element_type=f32))
    wide = middle.astype(f32)
    scaled_two = (wide * norm_second).astype(bf16)
    activation = jnp.dot(scaled_two, up_weight, preferred_element_type=f32).astype(bf16)
    hidden_dev = up_weight.shape[1]
    total = jnp.sum(wide * wide, axis=1, keepdims=True)
    high = lax.reduce_precision(total, 8, 7)
    mid = lax.reduce_precision(total - high, 8, 7)
    low = total - high - mid
    lane = lax.broadcasted_iota(jnp.int32, (rows, LANES), 1)
    columns = jnp.where(lane == 0, high, jnp.where(lane == 1, mid, jnp.where(lane == 2, low, 0.0))).astype(bf16)
    sent = jnp.concatenate([activation, columns], axis=1).reshape(peers, rows_dev, hidden_dev + LANES)
    sums = exchange(sent, REQ).astype(f32).sum(axis=0)
    squares = sums[:, hidden_dev : hidden_dev + 1] + sums[:, hidden_dev + 1 : hidden_dev + 2] + sums[:, hidden_dev + 2 : hidden_dev + 3]
    inverse = lax.rsqrt(squares / width_all + eps)
    hidden = jnp.square(jax.nn.relu(sums[:, :hidden_dev] * inverse)).astype(bf16)
    every_hidden = to_everyone(hidden, REQ)
    residual_out = add_over_heads(middle, jnp.dot(every_hidden, down_weight, preferred_element_type=f32))
    return residual_out, state_out, jnp.transpose(tail_mix_out, (1, 0, 2)), tail_group_out


def solution(mesh):
    devices = mesh.devices
    finer = Mesh(devices.reshape(4, devices.shape[0] // 4, devices.shape[1] // 2, 2), REQ + HEAD)
    placed = (
        P(None, REQ),
        P(REQ),
        P(REQ, HEAD, None, None),
        P(REQ, None, HEAD),
        P(REQ, None, None, HEAD),
        P(REQ),
        P(REQ, None, HEAD),
        P(REQ, None, HEAD),
        P(REQ, HEAD),
        P(None, HEAD),
        P(None, None, HEAD),
        P(HEAD),
        P(None, HEAD),
        P(HEAD),
        P(HEAD),
        P(HEAD),
        P(HEAD),
        P(HEAD, REQ),
        P(REQ),
        P(REQ, HEAD),
        P(HEAD, REQ),
    )
    return jax.shard_map(
        on_device,
        mesh=finer,
        in_specs=placed,
        out_specs=(P(None, REQ), P(REQ, HEAD, None, None), P(REQ, None, HEAD), P(REQ, None, None, HEAD)),
        check_vma=False,
    )
```

```python
import jax
import jax.numpy as jnp
from jax import lax
from jax.experimental import pallas as pl
from jax.experimental.pallas import tpu as pltpu
from jax.sharding import Mesh
from jax.sharding import PartitionSpec as P

REQ = ("z", "x")
HEAD = ("y", "c")
LANES = 128
BATCH = 4
IN_VMEM = pl.BlockSpec(memory_space=pltpu.VMEM)
SMALL = pltpu.CompilerParams(vmem_limit_bytes=16 * 2**20)
f32 = jnp.float32
bf16 = jnp.bfloat16

eps = 1e-05


def three_parts(total):
    high = total.astype(bf16)
    rest = total - high.astype(f32)
    middle = rest.astype(bf16)
    low = (rest - middle.astype(f32)).astype(bf16)
    return high, middle, low


def in_hbm(value):
    return pltpu.with_memory_space_constraint(value, pltpu.HBM)


def silu(v):
    return v / (1.0 + jnp.exp(-v))


def norm_columns(wide, width):
    total = jnp.sum(wide * wide, axis=1, keepdims=True)
    high, middle, low = three_parts(total)
    lane = lax.broadcasted_iota(jnp.int32, (wide.shape[0], LANES), 1)
    zero = jnp.zeros((wide.shape[0], LANES), f32)
    out = jnp.where(lane == width, high.astype(f32), zero)
    out = jnp.where(lane == width + 1, middle.astype(f32), out)
    return jnp.where(lane == width + 2, low.astype(f32), out)


def input_kernel(residual_ref, norm_ref, mix_ref, group_ref, step_ref, out_ref):
    wide = residual_ref[...].astype(f32)
    scaled = (wide * norm_ref[...]).astype(bf16)
    mix = mix_ref.shape[1]
    group = group_ref.shape[1]
    steps = step_ref.shape[0]
    out_ref[:, :mix] = jnp.dot(scaled, mix_ref[...], preferred_element_type=f32).astype(bf16)
    out_ref[:, mix : mix + group] = jnp.dot(scaled, group_ref[...], preferred_element_type=f32).astype(bf16)
    step = lax.dot_general(scaled, step_ref[...], (((1,), (1,)), ((), ())), preferred_element_type=f32)
    tail = norm_columns(wide, steps)
    out_ref[:, mix + group :] = tail.astype(bf16)
    out_ref[:, mix + group : mix + group + steps] = step.astype(bf16)


def input_projection(residual, norm, mix, group, step_t):
    rows = residual.shape[0]
    width = mix.shape[1] + group.shape[1] + LANES
    return pl.pallas_call(
        input_kernel,
        out_shape=jax.ShapeDtypeStruct((rows, width), bf16),
        in_specs=[IN_VMEM] * 5,
        out_specs=IN_VMEM,
        compiler_params=SMALL,
        name="input_projection",
    )(residual, norm, mix, group, step_t)


def expander(heads, mix, head_dim):
    row = lax.broadcasted_iota(jnp.int32, (heads, mix), 0)
    col = lax.broadcasted_iota(jnp.int32, (heads, mix), 1)
    return (col // head_dim == row).astype(f32)


def make_mixer_kernel(width_all, dims):
    pieces, rows, heads, head_dim, state, mix, taps = dims

    def kernel(
        arrived_ref, lengths_ref, tail_mix_ref, tail_group_ref, conv_mix_ref, conv_group_ref,
        bias_mix_ref, bias_group_ref, step_bias_ref, decay_log_ref, skip_ref, gain_ref, state_ref,
        y_ref, tail_mix_out_ref, tail_group_out_ref, u_ref, decay_ref, b_ref,
        c_ref, columns_ref, read_ref, buffer_ref, sems,
    ):
        def fetch(r):
            return pltpu.make_async_copy(state_ref.at[r], buffer_ref.at[r], sems.at[r])

        def begin(r, carry):
            fetch(r).start()
            return carry

        lax.fori_loop(0, rows, begin, 0)
        spread = expander(heads, mix, head_dim)

        def expand(v):
            return jnp.dot(v, spread, precision=lax.Precision.HIGHEST, preferred_element_type=f32)

        def total(lo, hi):
            acc = arrived_ref[0, :, lo:hi].astype(f32)
            for j in range(1, pieces):
                acc = acc + arrived_ref[j, :, lo:hi].astype(f32)
            return acc

        base = 2 * mix
        last = total(base + 2 * state, base + 2 * state + LANES)
        squares = last[:, heads : heads + 1] + last[:, heads + 1 : heads + 2] + last[:, heads + 2 : heads + 3]
        inverse = lax.rsqrt(squares / width_all + eps)
        across = jnp.broadcast_to(lengths_ref[...].astype(f32), (rows, rows))
        diagonal = lax.broadcasted_iota(jnp.int32, (rows, rows), 0) == lax.broadcasted_iota(jnp.int32, (rows, rows), 1)
        lengths = jnp.sum(jnp.where(diagonal, across, 0.0), axis=1, keepdims=True)
        valid = jnp.minimum(lengths, taps - 1.0)
        keep = [(valid >= taps - 1.0 - j).astype(f32) for j in range(taps - 1)]
        for g, dest in ((0, b_ref), (1, c_ref)):
            group_in = total(base + g * state, base + (g + 1) * state) * inverse
            conv = group_in * conv_group_ref[taps - 1, g : g + 1, :]
            for j in range(taps - 1):
                w = tail_group_ref[:, j, g, :] * keep[j]
                if j > 0:
                    tail_group_out_ref[:, j - 1, g, :] = w
                conv = conv + w * conv_group_ref[j, g : g + 1, :]
            tail_group_out_ref[:, taps - 2, g, :] = group_in
            dest[...] = silu(conv + bias_group_ref[g : g + 1, :])

        mix_in = total(mix, base) * inverse
        conv = mix_in * conv_mix_ref[taps - 1 : taps, :]
        for j in range(taps - 1):
            w = tail_mix_ref[j] * keep[j]
            if j > 0:
                tail_mix_out_ref[j - 1] = w
            conv = conv + w * conv_mix_ref[j : j + 1, :]
        tail_mix_out_ref[taps - 2] = mix_in
        x = silu(conv + bias_mix_ref[...])
        v = last[:, :heads] * inverse + step_bias_ref[...]
        step_size = jnp.maximum(v, 0.0) + jnp.log1p(jnp.exp(-jnp.abs(v)))
        alive = (lengths > 0.0).astype(f32)
        decay = jnp.exp(-step_size * jnp.exp(decay_log_ref[...])) * alive
        decay_ref[...] = jnp.concatenate([decay, jnp.zeros((rows, LANES - heads), f32)], axis=1)
        u = expand(step_size) * x
        for t in range(mix // LANES):
            u_ref[t] = u[:, t * LANES : (t + 1) * LANES]
        c = c_ref[...]
        c_high = c.astype(bf16).astype(f32)
        both = jnp.concatenate([c_high, c - c_high, jnp.zeros((LANES - 2 * rows, state), f32)], axis=0)
        columns_ref[...] = jnp.transpose(both)
        read_ref[...] = jnp.zeros_like(read_ref)
        lane = lax.broadcasted_iota(jnp.int32, (state, LANES), 1)

        def some_rows(i, carry):
            left = []
            right = []
            for k in range(BATCH):
                r = i * BATCH + k
                fetch(r).wait()
                s = buffer_ref[r].reshape(mix, state)
                s_high = s.astype(bf16)
                left += [s_high, (s - s_high.astype(f32)).astype(bf16)]
                own = jnp.where(lane % rows == r, columns_ref[...], 0.0).astype(bf16)
                right += [own, own]
            read_ref[...] += jnp.dot(
                jnp.concatenate(left, axis=1), jnp.concatenate(right, axis=0), preferred_element_type=f32
            )
            return carry

        lax.fori_loop(0, rows // BATCH, some_rows, 0)
        across_read = jnp.transpose(read_ref[...])
        read = across_read[:rows, :] + across_read[rows : 2 * rows, :]
        bc = jnp.sum(b_ref[...] * c_ref[...], axis=1, keepdims=True)
        skip = expand(jnp.broadcast_to(skip_ref[...], (rows, heads)))
        mixed = expand(decay) * read + u * bc + skip * x
        gated = mixed * silu(total(0, mix) * inverse)
        inverse_gated = lax.rsqrt(jnp.mean(gated * gated, axis=1, keepdims=True) + eps)
        y = (gated * inverse_gated * gain_ref[...]).astype(bf16)
        for j in range(pieces):
            y_ref[j] = y

    return kernel


def mixer_step(arrived, lengths, tail_mix, tail_group, conv_mix, conv_group, bias_mix, bias_group,
               step_bias, decay_log, skip_gain, gate_gain, ssm_state, width_all):
    pieces, rows, width = arrived.shape
    _, heads, head_dim, state = ssm_state.shape
    mix = heads * head_dim
    taps = conv_mix.shape[0]
    args = (
        arrived, lengths[None], jnp.transpose(tail_mix, (1, 0, 2)), tail_group, conv_mix, conv_group,
        bias_mix[None], bias_group, step_bias[None], decay_log[None], skip_gain[None], gate_gain[None], in_hbm(ssm_state),
    )
    outs = (
        jax.ShapeDtypeStruct((pieces, rows, mix), bf16),
        jax.ShapeDtypeStruct((taps - 1, rows, mix), f32),
        jax.ShapeDtypeStruct((rows, taps - 1, 2, state), f32),
        jax.ShapeDtypeStruct((mix // LANES, rows, LANES), f32),
        jax.ShapeDtypeStruct((rows, LANES), f32),
        jax.ShapeDtypeStruct((rows, state), f32),
    )
    return pl.pallas_call(
        make_mixer_kernel(width_all, (pieces, rows, heads, head_dim, state, mix, taps)),
        in_specs=[IN_VMEM] * (len(args) - 1) + [pl.BlockSpec(memory_space=pl.ANY)],
        out_specs=[IN_VMEM] * len(outs),
        out_shape=outs,
        scratch_shapes=[
            pltpu.VMEM((rows, state), f32),
            pltpu.VMEM((state, LANES), f32),
            pltpu.VMEM((mix, LANES), f32),
            pltpu.VMEM((rows, heads, head_dim, state), f32),
            pltpu.SemaphoreType.DMA((rows,)),
        ],
        compiler_params=SMALL,
        name="mixer_step",
    )(*args)


def make_update_kernel(rows, heads, head_dim, state):
    def kernel(u_ref, decay_ref, b_ref, state_ref, out_ref, buffer_ref, arrivals, departures):
        def fetch(r):
            return pltpu.make_async_copy(state_ref.at[r], buffer_ref.at[r], arrivals.at[r])

        def leave(r):
            return pltpu.make_async_copy(buffer_ref.at[r], out_ref.at[r], departures.at[r])

        def begin(r, carry):
            fetch(r).start()
            return carry

        lax.fori_loop(0, rows, begin, 0)

        def one_row(r, carry):
            fetch(r).wait()
            b_row = b_ref[pl.ds(r, 1), :]
            d_col = jnp.transpose(jnp.broadcast_to(decay_ref[pl.ds(r, 1), :], (LANES, LANES)))
            for h in range(heads):
                at = h * head_dim
                if at % LANES == 0:
                    u_row = u_ref[at // LANES, pl.ds(r, 1), :]
                    u_col = jnp.transpose(jnp.broadcast_to(u_row, (LANES, LANES)))
                u_h = u_col[at % LANES : at % LANES + head_dim, :]
                buffer_ref[r, h] = buffer_ref[r, h] * d_col[h : h + 1, :] + u_h * b_row
            leave(r).start()
            return carry

        lax.fori_loop(0, rows, one_row, 0)

        def finish(r, carry):
            leave(r).wait()
            return carry

        lax.fori_loop(0, rows, finish, 0)

    return kernel


def state_update(ssm_state, u, decay, b):
    rows, heads, head_dim, state = ssm_state.shape
    return pl.pallas_call(
        make_update_kernel(rows, heads, head_dim, state),
        in_specs=[IN_VMEM] * 3 + [pl.BlockSpec(memory_space=pl.ANY)],
        out_specs=pl.BlockSpec(memory_space=pl.ANY),
        out_shape=jax.ShapeDtypeStruct(ssm_state.shape, f32),
        scratch_shapes=[
            pltpu.VMEM(ssm_state.shape, f32),
            pltpu.SemaphoreType.DMA((rows,)),
            pltpu.SemaphoreType.DMA((rows,)),
        ],
        compiler_params=SMALL,
        name="state_update",
    )(u, decay, b, in_hbm(ssm_state))


def swap_core(value):
    return lax.ppermute(value, "c", [(0, 1), (1, 0)])


def ring_pairs(value, first):
    n = lax.axis_size("y")
    pairs = []
    for a in range(first, n + first, 2):
        p, q = a % n, (a + 1) % n
        pairs += [(p, q), (q, p)]
    return lax.ppermute(value, "y", pairs)


def head_sum_half(partial):
    half = partial.shape[0] // 2
    core = lax.axis_index("c")
    mine = lax.dynamic_slice_in_dim(partial, core * half, half, 0)
    theirs = lax.dynamic_slice_in_dim(partial, (1 - core) * half, half, 0).astype(bf16)
    total = mine + swap_core(theirs).astype(f32)
    for first in (0, 1):
        sent = total.astype(bf16)
        total = sent.astype(f32) + ring_pairs(sent, first).astype(f32)
    return total, core


def both_halves(half, core):
    other = swap_core(half)
    first = jnp.where(core == 0, half, other)
    second = jnp.where(core == 0, other, half)
    return jnp.concatenate([first, second], axis=0)


def add_over_heads(base, partial):
    total, core = head_sum_half(partial)
    half = total.shape[0]
    mine = lax.dynamic_slice_in_dim(base, core * half, half, 0).astype(f32)
    return both_halves((mine + total).astype(bf16), core)


def exchange(value, axis):
    return lax.all_to_all(value, axis, 0, 0, tiled=True)


def to_everyone(value, axis):
    peers = lax.axis_size(axis)
    copies = jnp.broadcast_to(value[None], (peers, *value.shape))
    return exchange(copies, axis).reshape(peers * value.shape[0], *value.shape[1:])


def on_device(
    residual, lengths, ssm_state, tail_mix, tail_group, norm_first, mix_weight, group_weight, step_weight,
    conv_mix, conv_group, bias_mix, bias_group, step_bias, decay_log, skip_gain, gate_gain, out_weight,
    norm_second, up_weight, down_weight,
):
    peers = lax.axis_size(REQ)
    rows_dev = ssm_state.shape[0]
    rows, width_dev = residual.shape
    width_all = width_dev * peers
    mix_flat = mix_weight.reshape(width_dev, -1)
    group_flat = group_weight.reshape(width_dev, -1)
    pieces = input_projection(residual, norm_first[None], mix_flat, group_flat, step_weight.T)
    arrived = exchange(pieces.reshape(peers, rows_dev, -1), REQ)
    copies, tail_mix_out, tail_group_out, u, decay, b = mixer_step(
        arrived, lengths, tail_mix, tail_group, conv_mix, conv_group, bias_mix, bias_group, step_bias,
        decay_log, skip_gain, gate_gain, ssm_state, width_all,
    )
    every_y = exchange(copies, REQ).reshape(rows, -1)
    state_out = state_update(ssm_state, u, decay, b)
    every_y, state_out = lax.optimization_barrier((every_y, state_out))
    middle = add_over_heads(residual, jnp.dot(every_y, out_weight, preferred_element_type=f32))
    wide = middle.astype(f32)
    scaled_two = (wide * norm_second).astype(bf16)
    activation = jnp.dot(scaled_two, up_weight, preferred_element_type=f32).astype(bf16)
    hidden_dev = up_weight.shape[1]
    total = jnp.sum(wide * wide, axis=1, keepdims=True)
    high = lax.reduce_precision(total, 8, 7)
    mid = lax.reduce_precision(total - high, 8, 7)
    low = total - high - mid
    lane = lax.broadcasted_iota(jnp.int32, (rows, LANES), 1)
    columns = jnp.where(lane == 0, high, jnp.where(lane == 1, mid, jnp.where(lane == 2, low, 0.0))).astype(bf16)
    sent = jnp.concatenate([activation, columns], axis=1).reshape(peers, rows_dev, hidden_dev + LANES)
    sums = exchange(sent, REQ).astype(f32).sum(axis=0)
    squares = sums[:, hidden_dev : hidden_dev + 1] + sums[:, hidden_dev + 1 : hidden_dev + 2] + sums[:, hidden_dev + 2 : hidden_dev + 3]
    inverse = lax.rsqrt(squares / width_all + eps)
    hidden = jnp.square(jax.nn.relu(sums[:, :hidden_dev] * inverse)).astype(bf16)
    every_hidden = to_everyone(hidden, REQ)
    residual_out = add_over_heads(middle, jnp.dot(every_hidden, down_weight, preferred_element_type=f32))
    return residual_out, state_out, jnp.transpose(tail_mix_out, (1, 0, 2)), tail_group_out


def solution(mesh):
    devices = mesh.devices
    finer = Mesh(devices.reshape(4, devices.shape[0] // 4, devices.shape[1] // 2, 2), REQ + HEAD)
    placed = (
        P(None, REQ),
        P(REQ),
        P(REQ, HEAD, None, None),
        P(REQ, None, HEAD),
        P(REQ, None, None, HEAD),
        P(REQ),
        P(REQ, None, HEAD),
        P(REQ, None, HEAD),
        P(REQ, HEAD),
        P(None, HEAD),
        P(None, None, HEAD),
        P(HEAD),
        P(None, HEAD),
        P(HEAD),
        P(HEAD),
        P(HEAD),
        P(HEAD),
        P(HEAD, REQ),
        P(REQ),
        P(REQ, HEAD),
        P(HEAD, REQ),
    )
    return jax.shard_map(
        on_device,
        mesh=finer,
        in_specs=placed,
        out_specs=(P(None, REQ), P(REQ, HEAD, None, None), P(REQ, None, HEAD), P(REQ, None, None, HEAD)),
        check_vma=False,
    )
```

```python
import jax
import jax.numpy as jnp
from jax import lax
from jax.experimental import pallas as pl
from jax.experimental.pallas import tpu as pltpu
from jax.sharding import Mesh
from jax.sharding import PartitionSpec as P

REQ = ("z", "x")
HEAD = ("y", "c")
LANES = 128
BATCH = 4
IN_VMEM = pl.BlockSpec(memory_space=pltpu.VMEM)
SMALL = pltpu.CompilerParams(vmem_limit_bytes=16 * 2**20)
f32 = jnp.float32
bf16 = jnp.bfloat16

eps = 1e-05


def three_parts(total):
    high = total.astype(bf16)
    rest = total - high.astype(f32)
    middle = rest.astype(bf16)
    low = (rest - middle.astype(f32)).astype(bf16)
    return high, middle, low


def in_hbm(value):
    return pltpu.with_memory_space_constraint(value, pltpu.HBM)


def silu(v):
    return v / (1.0 + jnp.exp(-v))


def norm_columns(wide, width):
    total = jnp.sum(wide * wide, axis=1, keepdims=True)
    high, middle, low = three_parts(total)
    lane = lax.broadcasted_iota(jnp.int32, (wide.shape[0], LANES), 1)
    zero = jnp.zeros((wide.shape[0], LANES), f32)
    out = jnp.where(lane == width, high.astype(f32), zero)
    out = jnp.where(lane == width + 1, middle.astype(f32), out)
    return jnp.where(lane == width + 2, low.astype(f32), out)


def input_kernel(residual_ref, norm_ref, mix_ref, group_ref, step_ref, out_ref):
    wide = residual_ref[...].astype(f32)
    scaled = (wide * norm_ref[...]).astype(bf16)
    mix = mix_ref.shape[1]
    group = group_ref.shape[1]
    steps = step_ref.shape[0]
    out_ref[:, :mix] = jnp.dot(scaled, mix_ref[...], preferred_element_type=f32).astype(bf16)
    out_ref[:, mix : mix + group] = jnp.dot(scaled, group_ref[...], preferred_element_type=f32).astype(bf16)
    step = lax.dot_general(scaled, step_ref[...], (((1,), (1,)), ((), ())), preferred_element_type=f32)
    tail = norm_columns(wide, steps)
    out_ref[:, mix + group :] = tail.astype(bf16)
    out_ref[:, mix + group : mix + group + steps] = step.astype(bf16)


def input_projection(residual, norm, mix, group, step_t):
    rows = residual.shape[0]
    width = mix.shape[1] + group.shape[1] + LANES
    return pl.pallas_call(
        input_kernel,
        out_shape=jax.ShapeDtypeStruct((rows, width), bf16),
        in_specs=[IN_VMEM] * 5,
        out_specs=IN_VMEM,
        compiler_params=SMALL,
        cost_estimate=pl.CostEstimate(flops=20_000_000_000, bytes_accessed=60_000_000, transcendentals=0),
        name="input_projection",
    )(residual, norm, mix, group, step_t)


def expander(heads, mix, head_dim):
    row = lax.broadcasted_iota(jnp.int32, (heads, mix), 0)
    col = lax.broadcasted_iota(jnp.int32, (heads, mix), 1)
    return (col // head_dim == row).astype(f32)


def make_mixer_kernel(width_all, dims):
    pieces, rows, heads, head_dim, state, mix, taps = dims

    def kernel(
        arrived_ref, lengths_ref, tail_mix_ref, tail_group_ref, conv_mix_ref, conv_group_ref,
        bias_mix_ref, bias_group_ref, step_bias_ref, decay_log_ref, skip_ref, gain_ref, state_ref,
        y_ref, tail_mix_out_ref, tail_group_out_ref, u_ref, decay_ref, b_ref,
        c_ref, columns_ref, read_ref,
    ):
        spread = expander(heads, mix, head_dim)

        def expand(v):
            return jnp.dot(v, spread, precision=lax.Precision.HIGHEST, preferred_element_type=f32)

        def total(lo, hi):
            acc = arrived_ref[0, :, lo:hi].astype(f32)
            for j in range(1, pieces):
                acc = acc + arrived_ref[j, :, lo:hi].astype(f32)
            return acc

        base = 2 * mix
        last = total(base + 2 * state, base + 2 * state + LANES)
        squares = last[:, heads : heads + 1] + last[:, heads + 1 : heads + 2] + last[:, heads + 2 : heads + 3]
        inverse = lax.rsqrt(squares / width_all + eps)
        across = jnp.broadcast_to(lengths_ref[...].astype(f32), (rows, rows))
        diagonal = lax.broadcasted_iota(jnp.int32, (rows, rows), 0) == lax.broadcasted_iota(jnp.int32, (rows, rows), 1)
        lengths = jnp.sum(jnp.where(diagonal, across, 0.0), axis=1, keepdims=True)
        valid = jnp.minimum(lengths, taps - 1.0)
        keep = [(valid >= taps - 1.0 - j).astype(f32) for j in range(taps - 1)]
        for g, dest in ((0, b_ref), (1, c_ref)):
            group_in = total(base + g * state, base + (g + 1) * state) * inverse
            conv = group_in * conv_group_ref[taps - 1, g : g + 1, :]
            for j in range(taps - 1):
                w = tail_group_ref[:, j, g, :] * keep[j]
                if j > 0:
                    tail_group_out_ref[:, j - 1, g, :] = w
                conv = conv + w * conv_group_ref[j, g : g + 1, :]
            tail_group_out_ref[:, taps - 2, g, :] = group_in
            dest[...] = silu(conv + bias_group_ref[g : g + 1, :])

        mix_in = total(mix, base) * inverse
        conv = mix_in * conv_mix_ref[taps - 1 : taps, :]
        for j in range(taps - 1):
            w = tail_mix_ref[j] * keep[j]
            if j > 0:
                tail_mix_out_ref[j - 1] = w
            conv = conv + w * conv_mix_ref[j : j + 1, :]
        tail_mix_out_ref[taps - 2] = mix_in
        x = silu(conv + bias_mix_ref[...])
        v = last[:, :heads] * inverse + step_bias_ref[...]
        step_size = jnp.maximum(v, 0.0) + jnp.log1p(jnp.exp(-jnp.abs(v)))
        alive = (lengths > 0.0).astype(f32)
        decay = jnp.exp(-step_size * jnp.exp(decay_log_ref[...])) * alive
        decay_ref[...] = jnp.concatenate([decay, jnp.zeros((rows, LANES - heads), f32)], axis=1)
        u = expand(step_size) * x
        for t in range(mix // LANES):
            u_ref[t] = u[:, t * LANES : (t + 1) * LANES]
        c = c_ref[...]
        c_high = c.astype(bf16).astype(f32)
        both = jnp.concatenate([c_high, c - c_high, jnp.zeros((LANES - 2 * rows, state), f32)], axis=0)
        columns_ref[...] = jnp.transpose(both)
        read_ref[...] = jnp.zeros_like(read_ref)
        lane = lax.broadcasted_iota(jnp.int32, (state, LANES), 1)

        def some_rows(i, carry):
            left = []
            right = []
            for k in range(BATCH):
                r = i * BATCH + k
                s = state_ref[r].reshape(mix, state)
                s_high = s.astype(bf16)
                left += [s_high, (s - s_high.astype(f32)).astype(bf16)]
                own = jnp.where(lane % rows == r, columns_ref[...], 0.0).astype(bf16)
                right += [own, own]
            read_ref[...] += jnp.dot(
                jnp.concatenate(left, axis=1), jnp.concatenate(right, axis=0), preferred_element_type=f32
            )
            return carry

        lax.fori_loop(0, rows // BATCH, some_rows, 0)
        across_read = jnp.transpose(read_ref[...])
        read = across_read[:rows, :] + across_read[rows : 2 * rows, :]
        bc = jnp.sum(b_ref[...] * c_ref[...], axis=1, keepdims=True)
        skip = expand(jnp.broadcast_to(skip_ref[...], (rows, heads)))
        mixed = expand(decay) * read + u * bc + skip * x
        gated = mixed * silu(total(0, mix) * inverse)
        inverse_gated = lax.rsqrt(jnp.mean(gated * gated, axis=1, keepdims=True) + eps)
        y = (gated * inverse_gated * gain_ref[...]).astype(bf16)
        for j in range(pieces):
            y_ref[j] = y

    return kernel


def mixer_step(arrived, lengths, tail_mix, tail_group, conv_mix, conv_group, bias_mix, bias_group,
               step_bias, decay_log, skip_gain, gate_gain, ssm_state, width_all):
    pieces, rows, width = arrived.shape
    _, heads, head_dim, state = ssm_state.shape
    mix = heads * head_dim
    taps = conv_mix.shape[0]
    args = (
        arrived, lengths[None], jnp.transpose(tail_mix, (1, 0, 2)), tail_group, conv_mix, conv_group,
        bias_mix[None], bias_group, step_bias[None], decay_log[None], skip_gain[None], gate_gain[None], ssm_state,
    )
    outs = (
        jax.ShapeDtypeStruct((pieces, rows, mix), bf16),
        jax.ShapeDtypeStruct((taps - 1, rows, mix), f32),
        jax.ShapeDtypeStruct((rows, taps - 1, 2, state), f32),
        jax.ShapeDtypeStruct((mix // LANES, rows, LANES), f32),
        jax.ShapeDtypeStruct((rows, LANES), f32),
        jax.ShapeDtypeStruct((rows, state), f32),
    )
    return pl.pallas_call(
        make_mixer_kernel(width_all, (pieces, rows, heads, head_dim, state, mix, taps)),
        in_specs=[IN_VMEM] * len(args),
        out_specs=[IN_VMEM] * len(outs),
        out_shape=outs,
        scratch_shapes=[
            pltpu.VMEM((rows, state), f32),
            pltpu.VMEM((state, LANES), f32),
            pltpu.VMEM((mix, LANES), f32),
        ],
        compiler_params=SMALL,
        name="mixer_step",
    )(*args)


def make_update_kernel(rows, heads, head_dim, state):
    def kernel(u_ref, decay_ref, b_ref, state_ref, out_ref, buffer_ref, arrivals, departures):
        def fetch(r):
            return pltpu.make_async_copy(state_ref.at[r], buffer_ref.at[r], arrivals.at[r])

        def leave(r):
            return pltpu.make_async_copy(buffer_ref.at[r], out_ref.at[r], departures.at[r])

        def begin(r, carry):
            fetch(r).start()
            return carry

        lax.fori_loop(0, rows, begin, 0)

        def one_row(r, carry):
            fetch(r).wait()
            b_row = b_ref[pl.ds(r, 1), :]
            d_col = jnp.transpose(jnp.broadcast_to(decay_ref[pl.ds(r, 1), :], (LANES, LANES)))
            for h in range(heads):
                at = h * head_dim
                if at % LANES == 0:
                    u_row = u_ref[at // LANES, pl.ds(r, 1), :]
                    u_col = jnp.transpose(jnp.broadcast_to(u_row, (LANES, LANES)))
                u_h = u_col[at % LANES : at % LANES + head_dim, :]
                buffer_ref[r, h] = buffer_ref[r, h] * d_col[h : h + 1, :] + u_h * b_row
            leave(r).start()
            return carry

        lax.fori_loop(0, rows, one_row, 0)

        def finish(r, carry):
            leave(r).wait()
            return carry

        lax.fori_loop(0, rows, finish, 0)

    return kernel


def state_update(ssm_state, u, decay, b):
    rows, heads, head_dim, state = ssm_state.shape
    return pl.pallas_call(
        make_update_kernel(rows, heads, head_dim, state),
        in_specs=[IN_VMEM] * 3 + [pl.BlockSpec(memory_space=pl.ANY)],
        out_specs=pl.BlockSpec(memory_space=pl.ANY),
        out_shape=jax.ShapeDtypeStruct(ssm_state.shape, f32),
        scratch_shapes=[
            pltpu.VMEM(ssm_state.shape, f32),
            pltpu.SemaphoreType.DMA((rows,)),
            pltpu.SemaphoreType.DMA((rows,)),
        ],
        compiler_params=SMALL,
        name="state_update",
    )(u, decay, b, in_hbm(ssm_state))


def swap_core(value):
    return lax.ppermute(value, "c", [(0, 1), (1, 0)])


def ring_pairs(value, first):
    n = lax.axis_size("y")
    pairs = []
    for a in range(first, n + first, 2):
        p, q = a % n, (a + 1) % n
        pairs += [(p, q), (q, p)]
    return lax.ppermute(value, "y", pairs)


def head_sum_half(partial):
    half = partial.shape[0] // 2
    core = lax.axis_index("c")
    mine = lax.dynamic_slice_in_dim(partial, core * half, half, 0)
    theirs = lax.dynamic_slice_in_dim(partial, (1 - core) * half, half, 0).astype(bf16)
    total = mine + swap_core(theirs).astype(f32)
    for first in (0, 1):
        sent = total.astype(bf16)
        total = sent.astype(f32) + ring_pairs(sent, first).astype(f32)
    return total, core


def both_halves(half, core):
    other = swap_core(half)
    first = jnp.where(core == 0, half, other)
    second = jnp.where(core == 0, other, half)
    return jnp.concatenate([first, second], axis=0)


def add_over_heads(base, partial):
    total, core = head_sum_half(partial)
    half = total.shape[0]
    mine = lax.dynamic_slice_in_dim(base, core * half, half, 0).astype(f32)
    return both_halves((mine + total).astype(bf16), core)


def exchange(value, axis):
    return lax.all_to_all(value, axis, 0, 0, tiled=True)


def to_everyone(value, axis):
    peers = lax.axis_size(axis)
    copies = jnp.broadcast_to(value[None], (peers, *value.shape))
    return exchange(copies, axis).reshape(peers * value.shape[0], *value.shape[1:])


def on_device(
    residual, lengths, ssm_state, tail_mix, tail_group, norm_first, mix_weight, group_weight, step_weight,
    conv_mix, conv_group, bias_mix, bias_group, step_bias, decay_log, skip_gain, gate_gain, out_weight,
    norm_second, up_weight, down_weight,
):
    peers = lax.axis_size(REQ)
    rows_dev = ssm_state.shape[0]
    rows, width_dev = residual.shape
    width_all = width_dev * peers
    mix_flat = mix_weight.reshape(width_dev, -1)
    group_flat = group_weight.reshape(width_dev, -1)
    pieces = input_projection(residual, norm_first[None], mix_flat, group_flat, step_weight.T)
    arrived = exchange(pieces.reshape(peers, rows_dev, -1), REQ)
    copies, tail_mix_out, tail_group_out, u, decay, b = mixer_step(
        arrived, lengths, tail_mix, tail_group, conv_mix, conv_group, bias_mix, bias_group, step_bias,
        decay_log, skip_gain, gate_gain, ssm_state, width_all,
    )
    every_y = exchange(copies, REQ).reshape(rows, -1)
    state_out = state_update(ssm_state, u, decay, b)
    every_y, state_out = lax.optimization_barrier((every_y, state_out))
    middle = add_over_heads(residual, jnp.dot(every_y, out_weight, preferred_element_type=f32))
    wide = middle.astype(f32)
    scaled_two = (wide * norm_second).astype(bf16)
    activation = jnp.dot(scaled_two, up_weight, preferred_element_type=f32).astype(bf16)
    hidden_dev = up_weight.shape[1]
    total = jnp.sum(wide * wide, axis=1, keepdims=True)
    high = lax.reduce_precision(total, 8, 7)
    mid = lax.reduce_precision(total - high, 8, 7)
    low = total - high - mid
    lane = lax.broadcasted_iota(jnp.int32, (rows, LANES), 1)
    columns = jnp.where(lane == 0, high, jnp.where(lane == 1, mid, jnp.where(lane == 2, low, 0.0))).astype(bf16)
    sent = jnp.concatenate([activation, columns], axis=1).reshape(peers, rows_dev, hidden_dev + LANES)
    sums = exchange(sent, REQ).astype(f32).sum(axis=0)
    squares = sums[:, hidden_dev : hidden_dev + 1] + sums[:, hidden_dev + 1 : hidden_dev + 2] + sums[:, hidden_dev + 2 : hidden_dev + 3]
    inverse = lax.rsqrt(squares / width_all + eps)
    hidden = jnp.square(jax.nn.relu(sums[:, :hidden_dev] * inverse)).astype(bf16)
    every_hidden = to_everyone(hidden, REQ)
    residual_out = add_over_heads(middle, jnp.dot(every_hidden, down_weight, preferred_element_type=f32))
    return residual_out, state_out, jnp.transpose(tail_mix_out, (1, 0, 2)), tail_group_out


def solution(mesh):
    devices = mesh.devices
    finer = Mesh(devices.reshape(4, devices.shape[0] // 4, devices.shape[1] // 2, 2), REQ + HEAD)
    placed = (
        P(None, REQ),
        P(REQ),
        P(REQ, HEAD, None, None),
        P(REQ, None, HEAD),
        P(REQ, None, None, HEAD),
        P(REQ),
        P(REQ, None, HEAD),
        P(REQ, None, HEAD),
        P(REQ, HEAD),
        P(None, HEAD),
        P(None, None, HEAD),
        P(HEAD),
        P(None, HEAD),
        P(HEAD),
        P(HEAD),
        P(HEAD),
        P(HEAD),
        P(HEAD, REQ),
        P(REQ),
        P(REQ, HEAD),
        P(HEAD, REQ),
    )
    return jax.shard_map(
        on_device,
        mesh=finer,
        in_specs=placed,
        out_specs=(P(None, REQ), P(REQ, HEAD, None, None), P(REQ, None, HEAD), P(REQ, None, None, HEAD)),
        check_vma=False,
    )
```

```python
import jax
import jax.numpy as jnp
from jax import lax
from jax.experimental import pallas as pl
from jax.experimental.pallas import tpu as pltpu
from jax.sharding import Mesh
from jax.sharding import PartitionSpec as P

REQ = ("z", "x")
HEAD = ("y", "c")
LANES = 128
BATCH = 8
ON_MXU = 3
IN_VMEM = pl.BlockSpec(memory_space=pltpu.VMEM)
SMALL = pltpu.CompilerParams(vmem_limit_bytes=16 * 2**20)
f32 = jnp.float32
bf16 = jnp.bfloat16

eps = 1e-05


def three_parts(total):
    high = total.astype(bf16)
    rest = total - high.astype(f32)
    middle = rest.astype(bf16)
    low = (rest - middle.astype(f32)).astype(bf16)
    return high, middle, low


def in_hbm(value):
    return pltpu.with_memory_space_constraint(value, pltpu.HBM)


def silu(v):
    return v / (1.0 + jnp.exp(-v))


def norm_columns(wide, width):
    total = jnp.sum(wide * wide, axis=1, keepdims=True)
    high, middle, low = three_parts(total)
    lane = lax.broadcasted_iota(jnp.int32, (wide.shape[0], LANES), 1)
    zero = jnp.zeros((wide.shape[0], LANES), f32)
    out = jnp.where(lane == width, high.astype(f32), zero)
    out = jnp.where(lane == width + 1, middle.astype(f32), out)
    return jnp.where(lane == width + 2, low.astype(f32), out)


def input_kernel(residual_ref, norm_ref, mix_ref, group_ref, step_ref, out_ref):
    wide = residual_ref[...].astype(f32)
    scaled = (wide * norm_ref[...]).astype(bf16)
    mix = mix_ref.shape[1]
    depth = wide.shape[1]
    state = group_ref.shape[2]
    group = 2 * state
    steps = step_ref.shape[0]
    out_ref[:, :mix] = jnp.dot(scaled, mix_ref[...], preferred_element_type=f32).astype(bf16)
    row = lax.broadcasted_iota(jnp.int32, (depth, 2 * depth), 0)
    col = lax.broadcasted_iota(jnp.int32, (depth, 2 * depth), 1)
    pairs = group_ref[...].reshape(2 * depth, state)
    for j in range(2):
        spaced = jnp.dot(scaled, (col == 2 * row + j).astype(bf16), preferred_element_type=f32).astype(bf16)
        at = mix + j * state
        out_ref[:, at : at + state] = jnp.dot(spaced, pairs, preferred_element_type=f32).astype(bf16)
    step = lax.dot_general(scaled, step_ref[...], (((1,), (1,)), ((), ())), preferred_element_type=f32)
    tail = norm_columns(wide, steps)
    out_ref[:, mix + group :] = tail.astype(bf16)
    out_ref[:, mix + group : mix + group + steps] = step.astype(bf16)


def input_projection(residual, norm, mix, group, step_t):
    rows = residual.shape[0]
    width = mix.shape[1] + 2 * group.shape[2] + LANES
    return pl.pallas_call(
        input_kernel,
        out_shape=jax.ShapeDtypeStruct((rows, width), bf16),
        in_specs=[IN_VMEM] * 5,
        out_specs=IN_VMEM,
        compiler_params=SMALL,
        cost_estimate=pl.CostEstimate(flops=20_000_000_000, bytes_accessed=60_000_000, transcendentals=0),
        name="input_projection",
    )(residual, norm, mix, group, step_t)


def expander(heads, mix, head_dim):
    row = lax.broadcasted_iota(jnp.int32, (heads, mix), 0)
    col = lax.broadcasted_iota(jnp.int32, (heads, mix), 1)
    return (col // head_dim == row).astype(f32)


def make_mixer_kernel(width_all, dims):
    pieces, rows, heads, head_dim, state, mix, taps = dims

    def kernel(
        arrived_ref, lengths_ref, tail_mix_ref, tail_group_ref, conv_mix_ref, conv_group_ref,
        bias_mix_ref, bias_group_ref, step_bias_ref, decay_log_ref, skip_ref, gain_ref, state_ref,
        y_ref, tail_mix_out_ref, tail_group_out_ref, u_ref, decay_ref, b_ref,
        c_ref, columns_ref, read_ref, summed_ref,
    ):
        spread = expander(heads, mix, head_dim)

        def expand(v):
            return jnp.dot(v, spread, precision=lax.Precision.HIGHEST, preferred_element_type=f32)

        def total(lo, hi):
            acc = arrived_ref[0, :, lo:hi].astype(f32)
            for j in range(1, pieces):
                acc = acc + arrived_ref[j, :, lo:hi].astype(f32)
            return acc

        base = 2 * mix
        last = total(base + 2 * state, base + 2 * state + LANES)
        squares = last[:, heads : heads + 1] + last[:, heads + 1 : heads + 2] + last[:, heads + 2 : heads + 3]
        inverse = lax.rsqrt(squares / width_all + eps)
        across = jnp.broadcast_to(lengths_ref[...].astype(f32), (rows, rows))
        diagonal = lax.broadcasted_iota(jnp.int32, (rows, rows), 0) == lax.broadcasted_iota(jnp.int32, (rows, rows), 1)
        lengths = jnp.sum(jnp.where(diagonal, across, 0.0), axis=1, keepdims=True)
        valid = jnp.minimum(lengths, taps - 1.0)
        keep = [(valid >= taps - 1.0 - j).astype(f32) for j in range(taps - 1)]
        for g, dest in ((0, b_ref), (1, c_ref)):
            group_in = total(base + g * state, base + (g + 1) * state) * inverse
            conv = group_in * conv_group_ref[taps - 1, g : g + 1, :]
            for j in range(taps - 1):
                w = tail_group_ref[:, j, g, :] * keep[j]
                if j > 0:
                    tail_group_out_ref[:, j - 1, g, :] = w
                conv = conv + w * conv_group_ref[j, g : g + 1, :]
            tail_group_out_ref[:, taps - 2, g, :] = group_in
            dest[...] = silu(conv + bias_group_ref[g : g + 1, :])

        mix_in = total(mix, base) * inverse
        conv = mix_in * conv_mix_ref[taps - 1 : taps, :]
        for j in range(taps - 1):
            w = tail_mix_ref[j] * keep[j]
            if j > 0:
                tail_mix_out_ref[j - 1] = w
            conv = conv + w * conv_mix_ref[j : j + 1, :]
        tail_mix_out_ref[taps - 2] = mix_in
        x = silu(conv + bias_mix_ref[...])
        v = last[:, :heads] * inverse + step_bias_ref[...]
        step_size = jnp.maximum(v, 0.0) + jnp.log1p(jnp.exp(-jnp.abs(v)))
        alive = (lengths > 0.0).astype(f32)
        decay = jnp.exp(-step_size * jnp.exp(decay_log_ref[...])) * alive
        decay_ref[...] = jnp.concatenate([decay, jnp.zeros((rows, LANES - heads), f32)], axis=1)
        u = expand(step_size) * x
        for t in range(mix // LANES):
            u_ref[t] = u[:, t * LANES : (t + 1) * LANES]
        c = c_ref[...]
        c_high = c.astype(bf16).astype(f32)
        both = jnp.concatenate([c_high, c - c_high, jnp.zeros((LANES - 2 * rows, state), f32)], axis=0)
        columns_ref[...] = jnp.transpose(both)
        read_ref[...] = jnp.zeros_like(read_ref)
        summed_ref[...] = jnp.zeros_like(summed_ref)
        head_lane = lax.broadcasted_iota(jnp.int32, (head_dim, LANES), 1)
        lane = lax.broadcasted_iota(jnp.int32, (state, LANES), 1)

        def some_rows(i, carry):
            left = []
            right = []
            others = []
            for k in range(BATCH):
                r = i * BATCH + k
                if k >= ON_MXU:
                    others.append((r, c_ref[pl.ds(r, 1), :]))
                    continue
                s = state_ref[r].reshape(mix, state)
                s_high = s.astype(bf16)
                left += [s_high, (s - s_high.astype(f32)).astype(bf16)]
                own = jnp.where(lane % rows == r, columns_ref[...], 0.0).astype(bf16)
                right += [own, own]
            read_ref[...] += jnp.dot(
                jnp.concatenate(left, axis=1), jnp.concatenate(right, axis=0), preferred_element_type=f32
            )
            for h in range(heads):
                at = slice(h * head_dim, (h + 1) * head_dim)
                block = summed_ref[at, :]
                for r, c_row in others:
                    part = jnp.sum(state_ref[r, h] * c_row, axis=1, keepdims=True)
                    block = jnp.where(head_lane == r, part, block)
                summed_ref[at, :] = block
            return carry

        lax.fori_loop(0, rows // BATCH, some_rows, 0)
        across_read = jnp.transpose(read_ref[...] + summed_ref[...])
        read = across_read[:rows, :] + across_read[rows : 2 * rows, :]
        bc = jnp.sum(b_ref[...] * c_ref[...], axis=1, keepdims=True)
        skip = expand(jnp.broadcast_to(skip_ref[...], (rows, heads)))
        mixed = expand(decay) * read + u * bc + skip * x
        gated = mixed * silu(total(0, mix) * inverse)
        inverse_gated = lax.rsqrt(jnp.mean(gated * gated, axis=1, keepdims=True) + eps)
        y = (gated * inverse_gated * gain_ref[...]).astype(bf16)
        for j in range(pieces):
            y_ref[j] = y

    return kernel


def mixer_step(arrived, lengths, tail_mix, tail_group, conv_mix, conv_group, bias_mix, bias_group,
               step_bias, decay_log, skip_gain, gate_gain, ssm_state, width_all):
    pieces, rows, width = arrived.shape
    _, heads, head_dim, state = ssm_state.shape
    mix = heads * head_dim
    taps = conv_mix.shape[0]
    args = (
        arrived, lengths[None], jnp.transpose(tail_mix, (1, 0, 2)), tail_group, conv_mix, conv_group,
        bias_mix[None], bias_group, step_bias[None], decay_log[None], skip_gain[None], gate_gain[None], ssm_state,
    )
    outs = (
        jax.ShapeDtypeStruct((pieces, rows, mix), bf16),
        jax.ShapeDtypeStruct((taps - 1, rows, mix), f32),
        jax.ShapeDtypeStruct((rows, taps - 1, 2, state), f32),
        jax.ShapeDtypeStruct((mix // LANES, rows, LANES), f32),
        jax.ShapeDtypeStruct((rows, LANES), f32),
        jax.ShapeDtypeStruct((rows, state), f32),
    )
    return pl.pallas_call(
        make_mixer_kernel(width_all, (pieces, rows, heads, head_dim, state, mix, taps)),
        in_specs=[IN_VMEM] * len(args),
        out_specs=[IN_VMEM] * len(outs),
        out_shape=outs,
        scratch_shapes=[
            pltpu.VMEM((rows, state), f32),
            pltpu.VMEM((state, LANES), f32),
            pltpu.VMEM((mix, LANES), f32),
            pltpu.VMEM((mix, LANES), f32),
        ],
        compiler_params=SMALL,
        name="mixer_step",
    )(*args)


def make_update_kernel(rows, heads, head_dim, state):
    def kernel(u_ref, decay_ref, b_ref, state_ref, out_ref, buffer_ref, arrivals, departures):
        def fetch(r):
            return pltpu.make_async_copy(state_ref.at[r], buffer_ref.at[r], arrivals.at[r])

        def leave(r):
            return pltpu.make_async_copy(buffer_ref.at[r], out_ref.at[r], departures.at[r])

        def begin(r, carry):
            fetch(r).start()
            return carry

        lax.fori_loop(0, rows, begin, 0)

        def one_row(r, carry):
            fetch(r).wait()
            b_row = b_ref[pl.ds(r, 1), :]
            d_col = jnp.transpose(jnp.broadcast_to(decay_ref[pl.ds(r, 1), :], (LANES, LANES)))
            for h in range(heads):
                at = h * head_dim
                if at % LANES == 0:
                    u_row = u_ref[at // LANES, pl.ds(r, 1), :]
                    u_col = jnp.transpose(jnp.broadcast_to(u_row, (LANES, LANES)))
                u_h = u_col[at % LANES : at % LANES + head_dim, :]
                buffer_ref[r, h] = buffer_ref[r, h] * d_col[h : h + 1, :] + u_h * b_row
            leave(r).start()
            return carry

        lax.fori_loop(0, rows, one_row, 0)

        def finish(r, carry):
            leave(r).wait()
            return carry

        lax.fori_loop(0, rows, finish, 0)

    return kernel


def state_update(ssm_state, u, decay, b):
    rows, heads, head_dim, state = ssm_state.shape
    return pl.pallas_call(
        make_update_kernel(rows, heads, head_dim, state),
        in_specs=[IN_VMEM] * 3 + [pl.BlockSpec(memory_space=pl.ANY)],
        out_specs=pl.BlockSpec(memory_space=pl.ANY),
        out_shape=jax.ShapeDtypeStruct(ssm_state.shape, f32),
        scratch_shapes=[
            pltpu.VMEM(ssm_state.shape, f32),
            pltpu.SemaphoreType.DMA((rows,)),
            pltpu.SemaphoreType.DMA((rows,)),
        ],
        compiler_params=SMALL,
        name="state_update",
    )(u, decay, b, in_hbm(ssm_state))


def up_kernel(middle_ref, norm_ref, up_ref, out_ref):
    wide = middle_ref[...].astype(f32)
    scaled = (wide * norm_ref[...]).astype(bf16)
    width = up_ref.shape[1]
    out_ref[:, width:] = norm_columns(wide, 0).astype(bf16)
    out_ref[:, :width] = jnp.dot(scaled, up_ref[...], preferred_element_type=f32).astype(bf16)


def up_projection(middle, norm, up):
    return pl.pallas_call(
        up_kernel,
        out_shape=jax.ShapeDtypeStruct((middle.shape[0], up.shape[1] + LANES), bf16),
        in_specs=[IN_VMEM] * 3,
        out_specs=IN_VMEM,
        compiler_params=SMALL,
        name="up_projection",
    )(middle, norm, up)


def swap_core(value):
    return lax.ppermute(value, "c", [(0, 1), (1, 0)])


def ring_pairs(value, first):
    n = lax.axis_size("y")
    pairs = []
    for a in range(first, n + first, 2):
        p, q = a % n, (a + 1) % n
        pairs += [(p, q), (q, p)]
    return lax.ppermute(value, "y", pairs)


def head_sum_half(partial):
    half = partial.shape[0] // 2
    core = lax.axis_index("c")
    mine = lax.dynamic_slice_in_dim(partial, core * half, half, 0)
    theirs = lax.dynamic_slice_in_dim(partial, (1 - core) * half, half, 0).astype(bf16)
    total = mine + swap_core(theirs).astype(f32)
    for first in (0, 1):
        sent = total.astype(bf16)
        total = sent.astype(f32) + ring_pairs(sent, first).astype(f32)
    return total, core


def both_halves(half, core):
    other = swap_core(half)
    first = jnp.where(core == 0, half, other)
    second = jnp.where(core == 0, other, half)
    return jnp.concatenate([first, second], axis=0)


def add_over_heads(base, partial):
    total, core = head_sum_half(partial)
    half = total.shape[0]
    mine = lax.dynamic_slice_in_dim(base, core * half, half, 0).astype(f32)
    return both_halves((mine + total).astype(bf16), core)


def exchange(value, axis):
    return lax.all_to_all(value, axis, 0, 0, tiled=True)


def to_everyone(value, axis):
    peers = lax.axis_size(axis)
    copies = jnp.broadcast_to(value[None], (peers, *value.shape))
    return exchange(copies, axis).reshape(peers * value.shape[0], *value.shape[1:])


def on_device(
    residual, lengths, ssm_state, tail_mix, tail_group, norm_first, mix_weight, group_weight, step_weight,
    conv_mix, conv_group, bias_mix, bias_group, step_bias, decay_log, skip_gain, gate_gain, out_weight,
    norm_second, up_weight, down_weight,
):
    peers = lax.axis_size(REQ)
    rows_dev = ssm_state.shape[0]
    rows, width_dev = residual.shape
    width_all = width_dev * peers
    mix_flat = mix_weight.reshape(width_dev, -1)
    pieces = input_projection(residual, norm_first[None], mix_flat, group_weight, step_weight.T)
    arrived = exchange(pieces.reshape(peers, rows_dev, -1), REQ)
    copies, tail_mix_out, tail_group_out, u, decay, b = mixer_step(
        arrived, lengths, tail_mix, tail_group, conv_mix, conv_group, bias_mix, bias_group, step_bias,
        decay_log, skip_gain, gate_gain, ssm_state, width_all,
    )
    every_y = exchange(copies, REQ).reshape(rows, -1)
    state_out = state_update(ssm_state, u, decay, b)
    every_y, state_out = lax.optimization_barrier((every_y, state_out))
    middle = add_over_heads(residual, jnp.dot(every_y, out_weight, preferred_element_type=f32))
    hidden_dev = up_weight.shape[1]
    sent = up_projection(middle, norm_second[None], up_weight).reshape(peers, rows_dev, -1)
    sums = exchange(sent, REQ).astype(f32).sum(axis=0)
    squares = sums[:, hidden_dev : hidden_dev + 1] + sums[:, hidden_dev + 1 : hidden_dev + 2] + sums[:, hidden_dev + 2 : hidden_dev + 3]
    inverse = lax.rsqrt(squares / width_all + eps)
    hidden = jnp.square(jax.nn.relu(sums[:, :hidden_dev] * inverse)).astype(bf16)
    every_hidden = to_everyone(hidden, REQ)
    residual_out = add_over_heads(middle, jnp.dot(every_hidden, down_weight, preferred_element_type=f32))
    return residual_out, state_out, jnp.transpose(tail_mix_out, (1, 0, 2)), tail_group_out


def solution(mesh):
    devices = mesh.devices
    finer = Mesh(devices.reshape(4, devices.shape[0] // 4, devices.shape[1] // 2, 2), REQ + HEAD)
    placed = (
        P(None, REQ),
        P(REQ),
        P(REQ, HEAD, None, None),
        P(REQ, None, HEAD),
        P(REQ, None, None, HEAD),
        P(REQ),
        P(REQ, None, HEAD),
        P(REQ, None, HEAD),
        P(REQ, HEAD),
        P(None, HEAD),
        P(None, None, HEAD),
        P(HEAD),
        P(None, HEAD),
        P(HEAD),
        P(HEAD),
        P(HEAD),
        P(HEAD),
        P(HEAD, REQ),
        P(REQ),
        P(REQ, HEAD),
        P(HEAD, REQ),
    )
    return jax.shard_map(
        on_device,
        mesh=finer,
        in_specs=placed,
        out_specs=(P(None, REQ), P(REQ, HEAD, None, None), P(REQ, None, HEAD), P(REQ, None, None, HEAD)),
        check_vma=False,
    )
```

```python
import jax
import jax.numpy as jnp
from jax import lax
from jax.experimental import pallas as pl
from jax.experimental.pallas import tpu as pltpu
from jax.sharding import Mesh
from jax.sharding import PartitionSpec as P

REQ = ("z", "x")
HEAD = ("y", "c")
LANES = 128
BATCH = 8
ON_MXU = 3
IN_VMEM = pl.BlockSpec(memory_space=pltpu.VMEM)
SMALL = pltpu.CompilerParams(vmem_limit_bytes=16 * 2**20)
f32 = jnp.float32
bf16 = jnp.bfloat16

eps = 1e-05


def three_parts(total):
    high = total.astype(bf16)
    rest = total - high.astype(f32)
    middle = rest.astype(bf16)
    low = (rest - middle.astype(f32)).astype(bf16)
    return high, middle, low


def in_hbm(value):
    return pltpu.with_memory_space_constraint(value, pltpu.HBM)


def silu(v):
    return v / (1.0 + jnp.exp(-v))


def norm_columns(wide, width):
    total = jnp.sum(wide * wide, axis=1, keepdims=True)
    high, middle, low = three_parts(total)
    lane = lax.broadcasted_iota(jnp.int32, (wide.shape[0], LANES), 1)
    zero = jnp.zeros((wide.shape[0], LANES), f32)
    out = jnp.where(lane == width, high.astype(f32), zero)
    out = jnp.where(lane == width + 1, middle.astype(f32), out)
    return jnp.where(lane == width + 2, low.astype(f32), out)


def input_kernel(residual_ref, norm_ref, mix_ref, group_ref, step_ref, out_ref):
    wide = residual_ref[...].astype(f32)
    scaled = (wide * norm_ref[...]).astype(bf16)
    mix = mix_ref.shape[1]
    depth = wide.shape[1]
    state = group_ref.shape[2]
    group = 2 * state
    steps = step_ref.shape[0]
    out_ref[:, :mix] = jnp.dot(scaled, mix_ref[...], preferred_element_type=f32).astype(bf16)
    row = lax.broadcasted_iota(jnp.int32, (depth, 2 * depth), 0)
    col = lax.broadcasted_iota(jnp.int32, (depth, 2 * depth), 1)
    pairs = group_ref[...].reshape(2 * depth, state)
    for j in range(2):
        spaced = jnp.dot(scaled, (col == 2 * row + j).astype(bf16), preferred_element_type=f32).astype(bf16)
        at = mix + j * state
        out_ref[:, at : at + state] = jnp.dot(spaced, pairs, preferred_element_type=f32).astype(bf16)
    step = lax.dot_general(scaled, step_ref[...], (((1,), (1,)), ((), ())), preferred_element_type=f32)
    tail = norm_columns(wide, steps)
    out_ref[:, mix + group :] = tail.astype(bf16)
    out_ref[:, mix + group : mix + group + steps] = step.astype(bf16)


def input_projection(residual, norm, mix, group, step_t):
    rows = residual.shape[0]
    width = mix.shape[1] + 2 * group.shape[2] + LANES
    return pl.pallas_call(
        input_kernel,
        out_shape=jax.ShapeDtypeStruct((rows, width), bf16),
        in_specs=[IN_VMEM] * 5,
        out_specs=IN_VMEM,
        compiler_params=SMALL,
        cost_estimate=pl.CostEstimate(flops=20_000_000_000, bytes_accessed=60_000_000, transcendentals=0),
        name="input_projection",
    )(residual, norm, mix, group, step_t)


def expander(heads, mix, head_dim):
    row = lax.broadcasted_iota(jnp.int32, (heads, mix), 0)
    col = lax.broadcasted_iota(jnp.int32, (heads, mix), 1)
    return (col // head_dim == row).astype(f32)


def make_mixer_kernel(width_all, dims):
    pieces, rows, heads, head_dim, state, mix, taps = dims

    def kernel(
        arrived_ref, lengths_ref, tail_mix_ref, tail_group_ref, conv_mix_ref, conv_group_ref,
        bias_mix_ref, bias_group_ref, step_bias_ref, decay_log_ref, skip_ref, gain_ref, state_ref,
        y_ref, tail_mix_out_ref, tail_group_out_ref, u_ref, decay_ref, b_ref,
        c_ref, columns_ref, read_ref, summed_ref,
    ):
        spread = expander(heads, mix, head_dim)

        def expand(v):
            return jnp.dot(v, spread, precision=lax.Precision.HIGHEST, preferred_element_type=f32)

        def total(lo, hi):
            acc = arrived_ref[0, :, lo:hi].astype(f32)
            for j in range(1, pieces):
                acc = acc + arrived_ref[j, :, lo:hi].astype(f32)
            return acc

        base = 2 * mix
        last = total(base + 2 * state, base + 2 * state + LANES)
        squares = last[:, heads : heads + 1] + last[:, heads + 1 : heads + 2] + last[:, heads + 2 : heads + 3]
        inverse = lax.rsqrt(squares / width_all + eps)
        across = jnp.broadcast_to(lengths_ref[...].astype(f32), (rows, rows))
        diagonal = lax.broadcasted_iota(jnp.int32, (rows, rows), 0) == lax.broadcasted_iota(jnp.int32, (rows, rows), 1)
        lengths = jnp.sum(jnp.where(diagonal, across, 0.0), axis=1, keepdims=True)
        valid = jnp.minimum(lengths, taps - 1.0)
        keep = [(valid >= taps - 1.0 - j).astype(f32) for j in range(taps - 1)]
        for g, dest in ((0, b_ref), (1, c_ref)):
            group_in = total(base + g * state, base + (g + 1) * state) * inverse
            conv = group_in * conv_group_ref[taps - 1, g : g + 1, :]
            for j in range(taps - 1):
                w = tail_group_ref[:, j, g, :] * keep[j]
                if j > 0:
                    tail_group_out_ref[:, j - 1, g, :] = w
                conv = conv + w * conv_group_ref[j, g : g + 1, :]
            tail_group_out_ref[:, taps - 2, g, :] = group_in
            dest[...] = silu(conv + bias_group_ref[g : g + 1, :])

        mix_in = total(mix, base) * inverse
        conv = mix_in * conv_mix_ref[taps - 1 : taps, :]
        for j in range(taps - 1):
            w = tail_mix_ref[j] * keep[j]
            if j > 0:
                tail_mix_out_ref[j - 1] = w
            conv = conv + w * conv_mix_ref[j : j + 1, :]
        tail_mix_out_ref[taps - 2] = mix_in
        x = silu(conv + bias_mix_ref[...])
        v = last[:, :heads] * inverse + step_bias_ref[...]
        step_size = jnp.maximum(v, 0.0) + jnp.log1p(jnp.exp(-jnp.abs(v)))
        alive = (lengths > 0.0).astype(f32)
        decay = jnp.exp(-step_size * jnp.exp(decay_log_ref[...])) * alive
        decay_ref[...] = jnp.concatenate([decay, jnp.zeros((rows, LANES - heads), f32)], axis=1)
        u = expand(step_size) * x
        for t in range(mix // LANES):
            u_ref[t] = u[:, t * LANES : (t + 1) * LANES]
        c = c_ref[...]
        c_high = c.astype(bf16).astype(f32)
        both = jnp.concatenate([c_high, c - c_high, jnp.zeros((LANES - 2 * rows, state), f32)], axis=0)
        columns_ref[...] = jnp.transpose(both)
        read_ref[...] = jnp.zeros_like(read_ref)
        summed_ref[...] = jnp.zeros_like(summed_ref)
        head_lane = lax.broadcasted_iota(jnp.int32, (head_dim, LANES), 1)
        lane = lax.broadcasted_iota(jnp.int32, (state, LANES), 1)

        def some_rows(i, carry):
            left = []
            right = []
            others = []
            for k in range(BATCH):
                r = i * BATCH + k
                if k >= ON_MXU:
                    others.append((r, c_ref[pl.ds(r, 1), :]))
                    continue
                s = state_ref[r].reshape(mix, state)
                s_high = s.astype(bf16)
                left += [s_high, (s - s_high.astype(f32)).astype(bf16)]
                own = jnp.where(lane % rows == r, columns_ref[...], 0.0).astype(bf16)
                right += [own, own]
            read_ref[...] += jnp.dot(
                jnp.concatenate(left, axis=1), jnp.concatenate(right, axis=0), preferred_element_type=f32
            )
            for h in range(heads):
                at = slice(h * head_dim, (h + 1) * head_dim)
                block = summed_ref[at, :]
                for r, c_row in others:
                    part = jnp.sum(state_ref[r, h] * c_row, axis=1, keepdims=True)
                    block = jnp.where(head_lane == r, part, block)
                summed_ref[at, :] = block
            return carry

        lax.fori_loop(0, rows // BATCH, some_rows, 0)
        across_read = jnp.transpose(read_ref[...] + summed_ref[...])
        read = across_read[:rows, :] + across_read[rows : 2 * rows, :]
        bc = jnp.sum(b_ref[...] * c_ref[...], axis=1, keepdims=True)
        skip = expand(jnp.broadcast_to(skip_ref[...], (rows, heads)))
        mixed = expand(decay) * read + u * bc + skip * x
        gated = mixed * silu(total(0, mix) * inverse)
        inverse_gated = lax.rsqrt(jnp.mean(gated * gated, axis=1, keepdims=True) + eps)
        y = (gated * inverse_gated * gain_ref[...]).astype(bf16)
        for j in range(pieces):
            y_ref[j] = y

    return kernel


def mixer_step(arrived, lengths, tail_mix, tail_group, conv_mix, conv_group, bias_mix, bias_group,
               step_bias, decay_log, skip_gain, gate_gain, ssm_state, width_all):
    pieces, rows, width = arrived.shape
    _, heads, head_dim, state = ssm_state.shape
    mix = heads * head_dim
    taps = conv_mix.shape[0]
    args = (
        arrived, lengths[None], jnp.transpose(tail_mix, (1, 0, 2)), tail_group, conv_mix, conv_group,
        bias_mix[None], bias_group, step_bias[None], decay_log[None], skip_gain[None], gate_gain[None], ssm_state,
    )
    outs = (
        jax.ShapeDtypeStruct((pieces, rows, mix), bf16),
        jax.ShapeDtypeStruct((taps - 1, rows, mix), f32),
        jax.ShapeDtypeStruct((rows, taps - 1, 2, state), f32),
        jax.ShapeDtypeStruct((mix // LANES, rows, LANES), f32),
        jax.ShapeDtypeStruct((rows, LANES), f32),
        jax.ShapeDtypeStruct((rows, state), f32),
    )
    return pl.pallas_call(
        make_mixer_kernel(width_all, (pieces, rows, heads, head_dim, state, mix, taps)),
        in_specs=[IN_VMEM] * len(args),
        out_specs=[IN_VMEM] * len(outs),
        out_shape=outs,
        scratch_shapes=[
            pltpu.VMEM((rows, state), f32),
            pltpu.VMEM((state, LANES), f32),
            pltpu.VMEM((mix, LANES), f32),
            pltpu.VMEM((mix, LANES), f32),
        ],
        compiler_params=SMALL,
        name="mixer_step",
    )(*args)


def make_update_kernel(rows, heads, head_dim, state):
    def kernel(u_ref, decay_ref, b_ref, state_ref, out_ref, buffer_ref, arrivals, departures):
        def fetch(r):
            return pltpu.make_async_copy(state_ref.at[r], buffer_ref.at[r], arrivals.at[r])

        def leave(r):
            return pltpu.make_async_copy(buffer_ref.at[r], out_ref.at[r], departures.at[r])

        def begin(r, carry):
            fetch(r).start()
            return carry

        lax.fori_loop(0, rows, begin, 0)

        def one_row(r, carry):
            fetch(r).wait()
            b_row = b_ref[pl.ds(r, 1), :]
            d_col = jnp.transpose(jnp.broadcast_to(decay_ref[pl.ds(r, 1), :], (LANES, LANES)))
            for h in range(heads):
                at = h * head_dim
                if at % LANES == 0:
                    u_row = u_ref[at // LANES, pl.ds(r, 1), :]
                    u_col = jnp.transpose(jnp.broadcast_to(u_row, (LANES, LANES)))
                u_h = u_col[at % LANES : at % LANES + head_dim, :]
                buffer_ref[r, h] = buffer_ref[r, h] * d_col[h : h + 1, :] + u_h * b_row
            leave(r).start()
            return carry

        lax.fori_loop(0, rows, one_row, 0)

        def finish(r, carry):
            leave(r).wait()
            return carry

        lax.fori_loop(0, rows, finish, 0)

    return kernel


def state_update(ssm_state, u, decay, b):
    rows, heads, head_dim, state = ssm_state.shape
    return pl.pallas_call(
        make_update_kernel(rows, heads, head_dim, state),
        in_specs=[IN_VMEM] * 3 + [pl.BlockSpec(memory_space=pl.ANY)],
        out_specs=pl.BlockSpec(memory_space=pl.ANY),
        out_shape=jax.ShapeDtypeStruct(ssm_state.shape, f32),
        scratch_shapes=[
            pltpu.VMEM(ssm_state.shape, f32),
            pltpu.SemaphoreType.DMA((rows,)),
            pltpu.SemaphoreType.DMA((rows,)),
        ],
        compiler_params=SMALL,
        name="state_update",
    )(u, decay, b, in_hbm(ssm_state))


def swap_core(value):
    return lax.ppermute(value, "c", [(0, 1), (1, 0)])


def ring_pairs(value, first):
    n = lax.axis_size("y")
    pairs = []
    for a in range(first, n + first, 2):
        p, q = a % n, (a + 1) % n
        pairs += [(p, q), (q, p)]
    return lax.ppermute(value, "y", pairs)


def head_sum_half(partial):
    half = partial.shape[0] // 2
    core = lax.axis_index("c")
    mine = lax.dynamic_slice_in_dim(partial, core * half, half, 0)
    theirs = lax.dynamic_slice_in_dim(partial, (1 - core) * half, half, 0).astype(bf16)
    total = mine + swap_core(theirs).astype(f32)
    for first in (0, 1):
        sent = total.astype(bf16)
        total = sent.astype(f32) + ring_pairs(sent, first).astype(f32)
    return total, core


def both_halves(half, core):
    other = swap_core(half)
    first = jnp.where(core == 0, half, other)
    second = jnp.where(core == 0, other, half)
    return jnp.concatenate([first, second], axis=0)


def add_over_heads(base, partial):
    total, core = head_sum_half(partial)
    half = total.shape[0]
    mine = lax.dynamic_slice_in_dim(base, core * half, half, 0).astype(f32)
    return both_halves((mine + total).astype(bf16), core)


def exchange(value, axis):
    return lax.all_to_all(value, axis, 0, 0, tiled=True)


def to_everyone(value, axis):
    peers = lax.axis_size(axis)
    copies = jnp.broadcast_to(value[None], (peers, *value.shape))
    return exchange(copies, axis).reshape(peers * value.shape[0], *value.shape[1:])


def on_device(
    residual, lengths, ssm_state, tail_mix, tail_group, norm_first, mix_weight, group_weight, step_weight,
    conv_mix, conv_group, bias_mix, bias_group, step_bias, decay_log, skip_gain, gate_gain, out_weight,
    norm_second, up_weight, down_weight,
):
    peers = lax.axis_size(REQ)
    rows_dev = ssm_state.shape[0]
    rows, width_dev = residual.shape
    width_all = width_dev * peers
    mix_flat = mix_weight.reshape(width_dev, -1)
    pieces = input_projection(residual, norm_first[None], mix_flat, group_weight, step_weight.T)
    arrived = exchange(pieces.reshape(peers, rows_dev, -1), REQ)
    copies, tail_mix_out, tail_group_out, u, decay, b = mixer_step(
        arrived, lengths, tail_mix, tail_group, conv_mix, conv_group, bias_mix, bias_group, step_bias,
        decay_log, skip_gain, gate_gain, ssm_state, width_all,
    )
    every_y = exchange(copies, REQ).reshape(rows, -1)
    state_out = state_update(ssm_state, u, decay, b)
    every_y, state_out = lax.optimization_barrier((every_y, state_out))
    middle = add_over_heads(residual, jnp.dot(every_y, out_weight, preferred_element_type=f32))
    wide = middle.astype(f32)
    scaled_two = (wide * norm_second).astype(bf16)
    activation = jnp.dot(scaled_two, up_weight, preferred_element_type=f32).astype(bf16)
    hidden_dev = up_weight.shape[1]
    total = jnp.sum(wide * wide, axis=1, keepdims=True)
    high = lax.reduce_precision(total, 8, 7)
    mid = lax.reduce_precision(total - high, 8, 7)
    low = total - high - mid
    lane = lax.broadcasted_iota(jnp.int32, (rows, LANES), 1)
    columns = jnp.where(lane == 0, high, jnp.where(lane == 1, mid, jnp.where(lane == 2, low, 0.0))).astype(bf16)
    sent = jnp.concatenate([activation, columns], axis=1).reshape(peers, rows_dev, hidden_dev + LANES)
    sums = exchange(sent, REQ).astype(f32).sum(axis=0)
    squares = sums[:, hidden_dev : hidden_dev + 1] + sums[:, hidden_dev + 1 : hidden_dev + 2] + sums[:, hidden_dev + 2 : hidden_dev + 3]
    inverse = lax.rsqrt(squares / width_all + eps)
    hidden = jnp.square(jax.nn.relu(sums[:, :hidden_dev] * inverse)).astype(bf16)
    every_hidden = to_everyone(hidden, REQ)
    residual_out = add_over_heads(middle, jnp.dot(every_hidden, down_weight, preferred_element_type=f32))
    return residual_out, state_out, jnp.transpose(tail_mix_out, (1, 0, 2)), tail_group_out


def solution(mesh):
    devices = mesh.devices
    finer = Mesh(devices.reshape(4, devices.shape[0] // 4, devices.shape[1] // 2, 2), REQ + HEAD)
    placed = (
        P(None, REQ),
        P(REQ),
        P(REQ, HEAD, None, None),
        P(REQ, None, HEAD),
        P(REQ, None, None, HEAD),
        P(REQ),
        P(REQ, None, HEAD),
        P(REQ, None, HEAD),
        P(REQ, HEAD),
        P(None, HEAD),
        P(None, None, HEAD),
        P(HEAD),
        P(None, HEAD),
        P(HEAD),
        P(HEAD),
        P(HEAD),
        P(HEAD),
        P(HEAD, REQ),
        P(REQ),
        P(REQ, HEAD),
        P(HEAD, REQ),
    )
    return jax.shard_map(
        on_device,
        mesh=finer,
        in_specs=placed,
        out_specs=(P(None, REQ), P(REQ, HEAD, None, None), P(REQ, None, HEAD), P(REQ, None, None, HEAD)),
        check_vma=False,
    )
```

```python
import jax
import jax.numpy as jnp
from jax import lax
from jax.experimental import pallas as pl
from jax.experimental.pallas import tpu as pltpu
from jax.sharding import Mesh
from jax.sharding import PartitionSpec as P

REQ = ("z", "x")
HEAD = ("y", "c")
LANES = 128
BATCH = 8
ON_MXU = 3
IN_VMEM = pl.BlockSpec(memory_space=pltpu.VMEM)
SMALL = pltpu.CompilerParams(vmem_limit_bytes=16 * 2**20)
f32 = jnp.float32
bf16 = jnp.bfloat16

eps = 1e-05


def three_parts(total):
    high = total.astype(bf16)
    rest = total - high.astype(f32)
    middle = rest.astype(bf16)
    low = (rest - middle.astype(f32)).astype(bf16)
    return high, middle, low


def in_hbm(value):
    return pltpu.with_memory_space_constraint(value, pltpu.HBM)


def silu(v):
    return v / (1.0 + jnp.exp(-v))


def norm_columns(wide, width):
    total = jnp.sum(wide * wide, axis=1, keepdims=True)
    high, middle, low = three_parts(total)
    lane = lax.broadcasted_iota(jnp.int32, (wide.shape[0], LANES), 1)
    zero = jnp.zeros((wide.shape[0], LANES), f32)
    out = jnp.where(lane == width, high.astype(f32), zero)
    out = jnp.where(lane == width + 1, middle.astype(f32), out)
    return jnp.where(lane == width + 2, low.astype(f32), out)


def input_kernel(residual_ref, norm_ref, mix_ref, group_ref, step_ref, out_ref):
    wide = residual_ref[...].astype(f32)
    scaled = (wide * norm_ref[...]).astype(bf16)
    mix = mix_ref.shape[1]
    depth = wide.shape[1]
    state = group_ref.shape[2]
    group = 2 * state
    steps = step_ref.shape[0]
    out_ref[:, :mix] = jnp.dot(scaled, mix_ref[...], preferred_element_type=f32).astype(bf16)
    row = lax.broadcasted_iota(jnp.int32, (depth, 2 * depth), 0)
    col = lax.broadcasted_iota(jnp.int32, (depth, 2 * depth), 1)
    pairs = group_ref[...].reshape(2 * depth, state)
    for j in range(2):
        spaced = jnp.dot(scaled, (col == 2 * row + j).astype(bf16), preferred_element_type=f32).astype(bf16)
        at = mix + j * state
        out_ref[:, at : at + state] = jnp.dot(spaced, pairs, preferred_element_type=f32).astype(bf16)
    step = lax.dot_general(scaled, step_ref[...], (((1,), (1,)), ((), ())), preferred_element_type=f32)
    tail = norm_columns(wide, steps)
    out_ref[:, mix + group :] = tail.astype(bf16)
    out_ref[:, mix + group : mix + group + steps] = step.astype(bf16)


def input_projection(residual, norm, mix, group, step_t):
    rows = residual.shape[0]
    width = mix.shape[1] + 2 * group.shape[2] + LANES
    return pl.pallas_call(
        input_kernel,
        out_shape=jax.ShapeDtypeStruct((rows, width), bf16),
        in_specs=[IN_VMEM] * 5,
        out_specs=IN_VMEM,
        compiler_params=SMALL,
        cost_estimate=pl.CostEstimate(flops=20_000_000_000, bytes_accessed=60_000_000, transcendentals=0),
        name="input_projection",
    )(residual, norm, mix, group, step_t)


def expander(heads, mix, head_dim):
    row = lax.broadcasted_iota(jnp.int32, (heads, mix), 0)
    col = lax.broadcasted_iota(jnp.int32, (heads, mix), 1)
    return (col // head_dim == row).astype(f32)


def make_mixer_kernel(width_all, dims):
    pieces, rows, heads, head_dim, state, mix, taps = dims

    def kernel(
        arrived_ref, lengths_ref, tail_mix_ref, tail_group_ref, conv_mix_ref, conv_group_ref,
        bias_mix_ref, bias_group_ref, step_bias_ref, decay_log_ref, skip_ref, gain_ref, state_ref,
        y_ref, tail_mix_out_ref, tail_group_out_ref, u_ref, decay_ref, b_ref,
        c_ref, columns_ref, read_ref, summed_ref,
    ):
        spread = expander(heads, mix, head_dim)

        def expand(v):
            return jnp.dot(v, spread, precision=lax.Precision.HIGHEST, preferred_element_type=f32)

        def total(lo, hi):
            acc = arrived_ref[0, :, lo:hi].astype(f32)
            for j in range(1, pieces):
                acc = acc + arrived_ref[j, :, lo:hi].astype(f32)
            return acc

        base = 2 * mix
        last = total(base + 2 * state, base + 2 * state + LANES)
        squares = last[:, heads : heads + 1] + last[:, heads + 1 : heads + 2] + last[:, heads + 2 : heads + 3]
        inverse = lax.rsqrt(squares / width_all + eps)
        across = jnp.broadcast_to(lengths_ref[...].astype(f32), (rows, rows))
        diagonal = lax.broadcasted_iota(jnp.int32, (rows, rows), 0) == lax.broadcasted_iota(jnp.int32, (rows, rows), 1)
        lengths = jnp.sum(jnp.where(diagonal, across, 0.0), axis=1, keepdims=True)
        valid = jnp.minimum(lengths, taps - 1.0)
        keep = [(valid >= taps - 1.0 - j).astype(f32) for j in range(taps - 1)]
        for g, dest in ((0, b_ref), (1, c_ref)):
            group_in = total(base + g * state, base + (g + 1) * state) * inverse
            conv = group_in * conv_group_ref[taps - 1, g : g + 1, :]
            for j in range(taps - 1):
                w = tail_group_ref[:, j, g, :] * keep[j]
                if j > 0:
                    tail_group_out_ref[:, j - 1, g, :] = w
                conv = conv + w * conv_group_ref[j, g : g + 1, :]
            tail_group_out_ref[:, taps - 2, g, :] = group_in
            dest[...] = silu(conv + bias_group_ref[g : g + 1, :])

        mix_in = total(mix, base) * inverse
        conv = mix_in * conv_mix_ref[taps - 1 : taps, :]
        for j in range(taps - 1):
            w = tail_mix_ref[j] * keep[j]
            if j > 0:
                tail_mix_out_ref[j - 1] = w
            conv = conv + w * conv_mix_ref[j : j + 1, :]
        tail_mix_out_ref[taps - 2] = mix_in
        x = silu(conv + bias_mix_ref[...])
        v = last[:, :heads] * inverse + step_bias_ref[...]
        step_size = jnp.maximum(v, 0.0) + jnp.log1p(jnp.exp(-jnp.abs(v)))
        alive = (lengths > 0.0).astype(f32)
        decay = jnp.exp(-step_size * jnp.exp(decay_log_ref[...])) * alive
        decay_ref[...] = jnp.concatenate([decay, jnp.zeros((rows, LANES - heads), f32)], axis=1)
        u = expand(step_size) * x
        for t in range(mix // LANES):
            u_ref[t] = u[:, t * LANES : (t + 1) * LANES]
        c = c_ref[...]
        c_high = c.astype(bf16).astype(f32)
        both = jnp.concatenate([c_high, c - c_high, jnp.zeros((LANES - 2 * rows, state), f32)], axis=0)
        columns_ref[...] = jnp.transpose(both)
        read_ref[...] = jnp.zeros_like(read_ref)
        summed_ref[...] = jnp.zeros_like(summed_ref)
        head_lane = lax.broadcasted_iota(jnp.int32, (head_dim, LANES), 1)
        lane = lax.broadcasted_iota(jnp.int32, (state, LANES), 1)

        def some_rows(i, carry):
            left = []
            right = []
            others = []
            for k in range(BATCH):
                r = i * BATCH + k
                if k >= ON_MXU:
                    others.append((r, c_ref[pl.ds(r, 1), :]))
                    continue
                s = state_ref[r].reshape(mix, state)
                s_high = s.astype(bf16)
                left += [s_high, (s - s_high.astype(f32)).astype(bf16)]
                own = jnp.where(lane % rows == r, columns_ref[...], 0.0).astype(bf16)
                right += [own, own]
            read_ref[...] += jnp.dot(
                jnp.concatenate(left, axis=1), jnp.concatenate(right, axis=0), preferred_element_type=f32
            )
            for h in range(heads):
                at = slice(h * head_dim, (h + 1) * head_dim)
                block = summed_ref[at, :]
                for r, c_row in others:
                    part = jnp.sum(state_ref[r, h] * c_row, axis=1, keepdims=True)
                    block = jnp.where(head_lane == r, part, block)
                summed_ref[at, :] = block
            return carry

        lax.fori_loop(0, rows // BATCH, some_rows, 0)
        across_read = jnp.transpose(read_ref[...] + summed_ref[...])
        read = across_read[:rows, :] + across_read[rows : 2 * rows, :]
        bc = jnp.sum(b_ref[...] * c_ref[...], axis=1, keepdims=True)
        skip = expand(jnp.broadcast_to(skip_ref[...], (rows, heads)))
        mixed = expand(decay) * read + u * bc + skip * x
        gated = mixed * silu(total(0, mix) * inverse)
        inverse_gated = lax.rsqrt(jnp.mean(gated * gated, axis=1, keepdims=True) + eps)
        y = (gated * inverse_gated * gain_ref[...]).astype(bf16)
        for j in range(pieces):
            y_ref[j] = y

    return kernel


def mixer_step(arrived, lengths, tail_mix, tail_group, conv_mix, conv_group, bias_mix, bias_group,
               step_bias, decay_log, skip_gain, gate_gain, ssm_state, width_all):
    pieces, rows, width = arrived.shape
    _, heads, head_dim, state = ssm_state.shape
    mix = heads * head_dim
    taps = conv_mix.shape[0]
    args = (
        arrived, lengths[None], jnp.transpose(tail_mix, (1, 0, 2)), tail_group, conv_mix, conv_group,
        bias_mix[None], bias_group, step_bias[None], decay_log[None], skip_gain[None], gate_gain[None], ssm_state,
    )
    outs = (
        jax.ShapeDtypeStruct((pieces, rows, mix), bf16),
        jax.ShapeDtypeStruct((taps - 1, rows, mix), f32),
        jax.ShapeDtypeStruct((rows, taps - 1, 2, state), f32),
        jax.ShapeDtypeStruct((mix // LANES, rows, LANES), f32),
        jax.ShapeDtypeStruct((rows, LANES), f32),
        jax.ShapeDtypeStruct((rows, state), f32),
    )
    return pl.pallas_call(
        make_mixer_kernel(width_all, (pieces, rows, heads, head_dim, state, mix, taps)),
        in_specs=[IN_VMEM] * len(args),
        out_specs=[IN_VMEM] * len(outs),
        out_shape=outs,
        scratch_shapes=[
            pltpu.VMEM((rows, state), f32),
            pltpu.VMEM((state, LANES), f32),
            pltpu.VMEM((mix, LANES), f32),
            pltpu.VMEM((mix, LANES), f32),
        ],
        compiler_params=SMALL,
        name="mixer_step",
    )(*args)


def make_update_kernel(rows, heads, head_dim, state):
    def kernel(u_ref, decay_ref, b_ref, state_ref, out_ref, buffer_ref, arrivals, departures):
        def fetch(r):
            return pltpu.make_async_copy(state_ref.at[r], buffer_ref.at[r], arrivals.at[r])

        def leave(r):
            return pltpu.make_async_copy(buffer_ref.at[r], out_ref.at[r], departures.at[r])

        def begin(r, carry):
            fetch(r).start()
            return carry

        lax.fori_loop(0, rows, begin, 0)

        def one_row(r, carry):
            fetch(r).wait()
            b_row = b_ref[pl.ds(r, 1), :]
            d_col = jnp.transpose(jnp.broadcast_to(decay_ref[pl.ds(r, 1), :], (LANES, LANES)))
            for h in range(heads):
                at = h * head_dim
                if at % LANES == 0:
                    u_row = u_ref[at // LANES, pl.ds(r, 1), :]
                    u_col = jnp.transpose(jnp.broadcast_to(u_row, (LANES, LANES)))
                u_h = u_col[at % LANES : at % LANES + head_dim, :]
                buffer_ref[r, h] = buffer_ref[r, h] * d_col[h : h + 1, :] + u_h * b_row
            leave(r).start()
            return carry

        lax.fori_loop(0, rows, one_row, 0)

        def finish(r, carry):
            leave(r).wait()
            return carry

        lax.fori_loop(0, rows, finish, 0)

    return kernel


def state_update(ssm_state, u, decay, b):
    rows, heads, head_dim, state = ssm_state.shape
    return pl.pallas_call(
        make_update_kernel(rows, heads, head_dim, state),
        in_specs=[IN_VMEM] * 3 + [pl.BlockSpec(memory_space=pl.ANY)],
        out_specs=pl.BlockSpec(memory_space=pl.ANY),
        out_shape=jax.ShapeDtypeStruct(ssm_state.shape, f32),
        scratch_shapes=[
            pltpu.VMEM(ssm_state.shape, f32),
            pltpu.SemaphoreType.DMA((rows,)),
            pltpu.SemaphoreType.DMA((rows,)),
        ],
        compiler_params=SMALL,
        name="state_update",
    )(u, decay, b, in_hbm(ssm_state))


def swap_core(value):
    return lax.ppermute(value, "c", [(0, 1), (1, 0)])


def ring_pairs(value, first):
    n = lax.axis_size("y")
    pairs = []
    for a in range(first, n + first, 2):
        p, q = a % n, (a + 1) % n
        pairs += [(p, q), (q, p)]
    return lax.ppermute(value, "y", pairs)


def ring_sum(total):
    for first in (0, 1):
        sent = total.astype(bf16)
        total = sent.astype(f32) + ring_pairs(sent, first).astype(f32)
    return total


def rows_from(value, start, count):
    return lax.dynamic_slice(value, (start, jnp.uint32(0)), (count, value.shape[1]))


def head_sum_half(partial, starts):
    half = partial.shape[0] // 2
    mine = rows_from(partial, starts[0], half)
    theirs = rows_from(partial, starts[1], half).astype(bf16)
    return ring_sum(mine + swap_core(theirs).astype(f32))


def both_halves(half, core, axis=0):
    other = swap_core(half)
    first = jnp.where(core == 0, half, other)
    second = jnp.where(core == 0, other, half)
    return jnp.concatenate([first, second], axis=axis)


def add_over_heads(base, partial, core, starts):
    total = head_sum_half(partial, starts)
    mine = rows_from(base, starts[0], total.shape[0]).astype(f32)
    return both_halves((mine + total).astype(bf16), core)


def of_core(value, core):
    return lax.dynamic_index_in_dim(value, core, 1, keepdims=False)


def add_mixer(residual, arrived, own_weight, other_weight, core):
    peers, _, rows, channels = arrived.shape
    own = of_core(arrived, core).reshape(peers * rows, channels)
    other = of_core(arrived, 1 - core).reshape(peers * rows, channels)
    partial = jnp.dot(own, own_weight, preferred_element_type=f32)
    total = ring_sum(partial + jnp.dot(other, other_weight, preferred_element_type=f32))
    mine = of_core(residual.reshape(peers, 2, rows, -1), core).reshape(peers * rows, -1).astype(f32)
    half = (mine + total).astype(bf16).reshape(peers, 1, rows, -1)
    return both_halves(half, core, 1).reshape(residual.shape)


def exchange(value, axis):
    return lax.all_to_all(value, axis, 0, 0, tiled=True)


def to_everyone(value, axis):
    peers = lax.axis_size(axis)
    copies = jnp.broadcast_to(value[None], (peers, *value.shape))
    return exchange(copies, axis).reshape(peers * value.shape[0], *value.shape[1:])


def on_device(
    residual, lengths, ssm_state, tail_mix, tail_group, norm_first, mix_weight, group_weight, step_weight,
    conv_mix, conv_group, bias_mix, bias_group, step_bias, decay_log, skip_gain, gate_gain, out_weight,
    norm_second, up_weight, down_weight,
):
    peers = lax.axis_size(REQ)
    rows_dev = ssm_state.shape[0]
    rows, width_dev = residual.shape
    width_all = width_dev * peers
    mix_flat = mix_weight.reshape(width_dev, -1)
    pieces = input_projection(residual, norm_first[None], mix_flat, group_weight, step_weight.T)
    other_weight = swap_core(out_weight)
    arrived = exchange(pieces.reshape(peers, rows_dev, -1), REQ)
    copies, tail_mix_out, tail_group_out, u, decay, b = mixer_step(
        arrived, lengths, tail_mix, tail_group, conv_mix, conv_group, bias_mix, bias_group, step_bias,
        decay_log, skip_gain, gate_gain, ssm_state, width_all,
    )
    every_y = exchange(copies.reshape(2 * peers, rows_dev // 2, -1), REQ + ("c",))
    state_out = state_update(ssm_state, u, decay, b)
    core = lax.axis_index("c")
    place = core.astype(jnp.uint32)
    starts = (place * jnp.uint32(rows // 2), (jnp.uint32(1) - place) * jnp.uint32(rows // 2))
    every_y, state_out, core, starts = lax.optimization_barrier((every_y, state_out, core, starts))
    every_y = every_y.reshape(peers, 2, rows_dev // 2, -1)
    middle = add_mixer(residual, every_y, out_weight, other_weight, core)
    wide = middle.astype(f32)
    scaled_two = (wide * norm_second).astype(bf16)
    activation = jnp.dot(scaled_two, up_weight, preferred_element_type=f32).astype(bf16)
    hidden_dev = up_weight.shape[1]
    total = jnp.sum(wide * wide, axis=1, keepdims=True)
    high = lax.reduce_precision(total, 8, 7)
    mid = lax.reduce_precision(total - high, 8, 7)
    low = total - high - mid
    lane = lax.broadcasted_iota(jnp.int32, (rows, LANES), 1)
    columns = jnp.where(lane == 0, high, jnp.where(lane == 1, mid, jnp.where(lane == 2, low, 0.0))).astype(bf16)
    sent = jnp.concatenate([activation, columns], axis=1).reshape(peers, rows_dev, hidden_dev + LANES)
    sums = exchange(sent, REQ).astype(f32).sum(axis=0)
    squares = sums[:, hidden_dev : hidden_dev + 1] + sums[:, hidden_dev + 1 : hidden_dev + 2] + sums[:, hidden_dev + 2 : hidden_dev + 3]
    inverse = lax.rsqrt(squares / width_all + eps)
    hidden = jnp.square(jax.nn.relu(sums[:, :hidden_dev] * inverse)).astype(bf16)
    every_hidden = to_everyone(hidden, REQ)
    projected = jnp.dot(every_hidden, down_weight, preferred_element_type=f32)
    residual_out = add_over_heads(middle, projected, core, starts)
    return residual_out, state_out, jnp.transpose(tail_mix_out, (1, 0, 2)), tail_group_out


def solution(mesh):
    devices = mesh.devices
    finer = Mesh(devices.reshape(4, devices.shape[0] // 4, devices.shape[1] // 2, 2), REQ + HEAD)
    placed = (
        P(None, REQ),
        P(REQ),
        P(REQ, HEAD, None, None),
        P(REQ, None, HEAD),
        P(REQ, None, None, HEAD),
        P(REQ),
        P(REQ, None, HEAD),
        P(REQ, None, HEAD),
        P(REQ, HEAD),
        P(None, HEAD),
        P(None, None, HEAD),
        P(HEAD),
        P(None, HEAD),
        P(HEAD),
        P(HEAD),
        P(HEAD),
        P(HEAD),
        P(HEAD, REQ),
        P(REQ),
        P(REQ, HEAD),
        P(HEAD, REQ),
    )
    return jax.shard_map(
        on_device,
        mesh=finer,
        in_specs=placed,
        out_specs=(P(None, REQ), P(REQ, HEAD, None, None), P(REQ, None, HEAD), P(REQ, None, None, HEAD)),
        check_vma=False,
    )
```

```python
import jax
import jax.numpy as jnp
from jax import lax
from jax.experimental import pallas as pl
from jax.experimental.pallas import tpu as pltpu
from jax.sharding import Mesh
from jax.sharding import PartitionSpec as P

REQ = ("z", "x")
HEAD = ("y", "c")
LANES = 128
BATCH = 8
ON_MXU = 5
IN_VMEM = pl.BlockSpec(memory_space=pltpu.VMEM)
SMALL = pltpu.CompilerParams(vmem_limit_bytes=16 * 2**20)
f32 = jnp.float32
bf16 = jnp.bfloat16

eps = 1e-05


def three_parts(total):
    high = total.astype(bf16)
    rest = total - high.astype(f32)
    middle = rest.astype(bf16)
    low = (rest - middle.astype(f32)).astype(bf16)
    return high, middle, low


def in_hbm(value):
    return pltpu.with_memory_space_constraint(value, pltpu.HBM)


def silu(v):
    return v / (1.0 + jnp.exp(-v))


def norm_columns(wide, width):
    total = jnp.sum(wide * wide, axis=1, keepdims=True)
    high, middle, low = three_parts(total)
    lane = lax.broadcasted_iota(jnp.int32, (wide.shape[0], LANES), 1)
    zero = jnp.zeros((wide.shape[0], LANES), f32)
    out = jnp.where(lane == width, high.astype(f32), zero)
    out = jnp.where(lane == width + 1, middle.astype(f32), out)
    return jnp.where(lane == width + 2, low.astype(f32), out)


def input_kernel(residual_ref, norm_ref, mix_ref, group_ref, step_ref, out_ref):
    wide = residual_ref[...].astype(f32)
    scaled = (wide * norm_ref[...]).astype(bf16)
    mix = mix_ref.shape[1]
    depth = wide.shape[1]
    state = group_ref.shape[2]
    group = 2 * state
    steps = step_ref.shape[0]
    out_ref[:, :mix] = jnp.dot(scaled, mix_ref[...], preferred_element_type=f32).astype(bf16)
    row = lax.broadcasted_iota(jnp.int32, (depth, 2 * depth), 0)
    col = lax.broadcasted_iota(jnp.int32, (depth, 2 * depth), 1)
    pairs = group_ref[...].reshape(2 * depth, state)
    for j in range(2):
        spaced = jnp.dot(scaled, (col == 2 * row + j).astype(bf16), preferred_element_type=f32).astype(bf16)
        at = mix + j * state
        out_ref[:, at : at + state] = jnp.dot(spaced, pairs, preferred_element_type=f32).astype(bf16)
    step = lax.dot_general(scaled, step_ref[...], (((1,), (1,)), ((), ())), preferred_element_type=f32)
    tail = norm_columns(wide, steps)
    out_ref[:, mix + group :] = tail.astype(bf16)
    out_ref[:, mix + group : mix + group + steps] = step.astype(bf16)


def input_projection(residual, norm, mix, group, step_t):
    rows = residual.shape[0]
    width = mix.shape[1] + 2 * group.shape[2] + LANES
    return pl.pallas_call(
        input_kernel,
        out_shape=jax.ShapeDtypeStruct((rows, width), bf16),
        in_specs=[IN_VMEM] * 5,
        out_specs=IN_VMEM,
        compiler_params=SMALL,
        cost_estimate=pl.CostEstimate(flops=20_000_000_000, bytes_accessed=60_000_000, transcendentals=0),
        name="input_projection",
    )(residual, norm, mix, group, step_t)


def expander(heads, mix, head_dim):
    row = lax.broadcasted_iota(jnp.int32, (heads, mix), 0)
    col = lax.broadcasted_iota(jnp.int32, (heads, mix), 1)
    return (col // head_dim == row).astype(f32)


def make_mixer_kernel(width_all, dims):
    pieces, rows, heads, head_dim, state, mix, taps = dims

    def kernel(
        arrived_ref, lengths_ref, tail_mix_ref, tail_group_ref, conv_mix_ref, conv_group_ref,
        bias_mix_ref, bias_group_ref, step_bias_ref, decay_log_ref, skip_ref, gain_ref, state_ref,
        y_ref, tail_mix_out_ref, tail_group_out_ref, u_ref, decay_ref, b_ref,
        c_ref, columns_ref, read_ref, summed_ref,
    ):
        spread = expander(heads, mix, head_dim)

        def expand(v):
            return jnp.dot(v, spread, precision=lax.Precision.HIGHEST, preferred_element_type=f32)

        def total(lo, hi):
            acc = arrived_ref[0, :, lo:hi].astype(f32)
            for j in range(1, pieces):
                acc = acc + arrived_ref[j, :, lo:hi].astype(f32)
            return acc

        base = 2 * mix
        last = total(base + 2 * state, base + 2 * state + LANES)
        squares = last[:, heads : heads + 1] + last[:, heads + 1 : heads + 2] + last[:, heads + 2 : heads + 3]
        inverse = lax.rsqrt(squares / width_all + eps)
        across = jnp.broadcast_to(lengths_ref[...].astype(f32), (rows, rows))
        diagonal = lax.broadcasted_iota(jnp.int32, (rows, rows), 0) == lax.broadcasted_iota(jnp.int32, (rows, rows), 1)
        lengths = jnp.sum(jnp.where(diagonal, across, 0.0), axis=1, keepdims=True)
        valid = jnp.minimum(lengths, taps - 1.0)
        keep = [(valid >= taps - 1.0 - j).astype(f32) for j in range(taps - 1)]
        for g, dest in ((0, b_ref), (1, c_ref)):
            group_in = total(base + g * state, base + (g + 1) * state) * inverse
            conv = group_in * conv_group_ref[taps - 1, g : g + 1, :]
            for j in range(taps - 1):
                w = tail_group_ref[:, j, g, :] * keep[j]
                if j > 0:
                    tail_group_out_ref[:, j - 1, g, :] = w
                conv = conv + w * conv_group_ref[j, g : g + 1, :]
            tail_group_out_ref[:, taps - 2, g, :] = group_in
            dest[...] = silu(conv + bias_group_ref[g : g + 1, :])

        mix_in = total(mix, base) * inverse
        conv = mix_in * conv_mix_ref[taps - 1 : taps, :]
        for j in range(taps - 1):
            w = tail_mix_ref[j] * keep[j]
            if j > 0:
                tail_mix_out_ref[j - 1] = w
            conv = conv + w * conv_mix_ref[j : j + 1, :]
        tail_mix_out_ref[taps - 2] = mix_in
        x = silu(conv + bias_mix_ref[...])
        v = last[:, :heads] * inverse + step_bias_ref[...]
        step_size = jnp.maximum(v, 0.0) + jnp.log1p(jnp.exp(-jnp.abs(v)))
        alive = (lengths > 0.0).astype(f32)
        decay = jnp.exp(-step_size * jnp.exp(decay_log_ref[...])) * alive
        decay_ref[...] = jnp.concatenate([decay, jnp.zeros((rows, LANES - heads), f32)], axis=1)
        u = expand(step_size) * x
        for t in range(mix // LANES):
            u_ref[t] = u[:, t * LANES : (t + 1) * LANES]
        c = c_ref[...]
        c_high = c.astype(bf16).astype(f32)
        both = jnp.concatenate([c_high, c - c_high, jnp.zeros((LANES - 2 * rows, state), f32)], axis=0)
        columns_ref[...] = jnp.transpose(both)
        read_ref[...] = jnp.zeros_like(read_ref)
        summed_ref[...] = jnp.zeros_like(summed_ref)
        head_lane = lax.broadcasted_iota(jnp.int32, (head_dim, LANES), 1)
        lane = lax.broadcasted_iota(jnp.int32, (state, LANES), 1)

        def some_rows(i, carry):
            left = []
            right = []
            others = []
            for k in range(BATCH):
                r = i * BATCH + k
                if k >= ON_MXU:
                    others.append((r, c_ref[pl.ds(r, 1), :]))
                    continue
                left.append(state_ref[r].reshape(mix, state).astype(bf16))
                right.append(jnp.where(lane % rows == r, columns_ref[...], 0.0).astype(bf16))
            read_ref[...] += jnp.dot(
                jnp.concatenate(left, axis=1), jnp.concatenate(right, axis=0), preferred_element_type=f32
            )
            for h in range(heads):
                at = slice(h * head_dim, (h + 1) * head_dim)
                block = summed_ref[at, :]
                for r, c_row in others:
                    part = jnp.sum(state_ref[r, h] * c_row, axis=1, keepdims=True)
                    block = jnp.where(head_lane == r, part, block)
                summed_ref[at, :] = block
            return carry

        lax.fori_loop(0, rows // BATCH, some_rows, 0)
        across_read = jnp.transpose(read_ref[...] + summed_ref[...])
        read = across_read[:rows, :] + across_read[rows : 2 * rows, :]
        bc = jnp.sum(b_ref[...] * c_ref[...], axis=1, keepdims=True)
        skip = expand(jnp.broadcast_to(skip_ref[...], (rows, heads)))
        mixed = expand(decay) * read + u * bc + skip * x
        gated = mixed * silu(total(0, mix) * inverse)
        inverse_gated = lax.rsqrt(jnp.mean(gated * gated, axis=1, keepdims=True) + eps)
        y = (gated * inverse_gated * gain_ref[...]).astype(bf16)
        for j in range(pieces):
            y_ref[j] = y

    return kernel


def mixer_step(arrived, lengths, tail_mix, tail_group, conv_mix, conv_group, bias_mix, bias_group,
               step_bias, decay_log, skip_gain, gate_gain, ssm_state, width_all):
    pieces, rows, width = arrived.shape
    _, heads, head_dim, state = ssm_state.shape
    mix = heads * head_dim
    taps = conv_mix.shape[0]
    args = (
        arrived, lengths[None], jnp.transpose(tail_mix, (1, 0, 2)), tail_group, conv_mix, conv_group,
        bias_mix[None], bias_group, step_bias[None], decay_log[None], skip_gain[None], gate_gain[None], ssm_state,
    )
    outs = (
        jax.ShapeDtypeStruct((pieces, rows, mix), bf16),
        jax.ShapeDtypeStruct((taps - 1, rows, mix), f32),
        jax.ShapeDtypeStruct((rows, taps - 1, 2, state), f32),
        jax.ShapeDtypeStruct((mix // LANES, rows, LANES), f32),
        jax.ShapeDtypeStruct((rows, LANES), f32),
        jax.ShapeDtypeStruct((rows, state), f32),
    )
    return pl.pallas_call(
        make_mixer_kernel(width_all, (pieces, rows, heads, head_dim, state, mix, taps)),
        in_specs=[IN_VMEM] * len(args),
        out_specs=[IN_VMEM] * len(outs),
        out_shape=outs,
        scratch_shapes=[
            pltpu.VMEM((rows, state), f32),
            pltpu.VMEM((state, LANES), f32),
            pltpu.VMEM((mix, LANES), f32),
            pltpu.VMEM((mix, LANES), f32),
        ],
        compiler_params=SMALL,
        name="mixer_step",
    )(*args)


def make_update_kernel(rows, heads, head_dim, state):
    def kernel(u_ref, decay_ref, b_ref, state_ref, out_ref, buffer_ref, arrivals, departures):
        def fetch(r):
            return pltpu.make_async_copy(state_ref.at[r], buffer_ref.at[r], arrivals.at[r])

        def leave(r):
            return pltpu.make_async_copy(buffer_ref.at[r], out_ref.at[r], departures.at[r])

        def begin(r, carry):
            fetch(r).start()
            return carry

        lax.fori_loop(0, rows, begin, 0)

        def one_row(r, carry):
            fetch(r).wait()
            b_row = b_ref[pl.ds(r, 1), :]
            d_col = jnp.transpose(jnp.broadcast_to(decay_ref[pl.ds(r, 1), :], (LANES, LANES)))
            for h in range(heads):
                at = h * head_dim
                if at % LANES == 0:
                    u_row = u_ref[at // LANES, pl.ds(r, 1), :]
                    u_col = jnp.transpose(jnp.broadcast_to(u_row, (LANES, LANES)))
                u_h = u_col[at % LANES : at % LANES + head_dim, :]
                buffer_ref[r, h] = buffer_ref[r, h] * d_col[h : h + 1, :] + u_h * b_row
            leave(r).start()
            return carry

        lax.fori_loop(0, rows, one_row, 0)

        def finish(r, carry):
            leave(r).wait()
            return carry

        lax.fori_loop(0, rows, finish, 0)

    return kernel


def state_update(ssm_state, u, decay, b):
    rows, heads, head_dim, state = ssm_state.shape
    return pl.pallas_call(
        make_update_kernel(rows, heads, head_dim, state),
        in_specs=[IN_VMEM] * 3 + [pl.BlockSpec(memory_space=pl.ANY)],
        out_specs=pl.BlockSpec(memory_space=pl.ANY),
        out_shape=jax.ShapeDtypeStruct(ssm_state.shape, f32),
        scratch_shapes=[
            pltpu.VMEM(ssm_state.shape, f32),
            pltpu.SemaphoreType.DMA((rows,)),
            pltpu.SemaphoreType.DMA((rows,)),
        ],
        compiler_params=SMALL,
        name="state_update",
    )(u, decay, b, in_hbm(ssm_state))


def swap_core(value):
    return lax.ppermute(value, "c", [(0, 1), (1, 0)])


def ring_pairs(value, first):
    n = lax.axis_size("y")
    pairs = []
    for a in range(first, n + first, 2):
        p, q = a % n, (a + 1) % n
        pairs += [(p, q), (q, p)]
    return lax.ppermute(value, "y", pairs)


def ring_sum(total):
    for first in (0, 1):
        sent = total.astype(bf16)
        total = sent.astype(f32) + ring_pairs(sent, first).astype(f32)
    return total


def rows_from(value, start, count):
    return lax.dynamic_slice(value, (start, jnp.uint32(0)), (count, value.shape[1]))


def head_sum_half(partial, starts):
    half = partial.shape[0] // 2
    mine = rows_from(partial, starts[0], half)
    theirs = rows_from(partial, starts[1], half).astype(bf16)
    return ring_sum(mine + swap_core(theirs).astype(f32))


def both_halves(half, core, axis=0):
    other = swap_core(half)
    first = jnp.where(core == 0, half, other)
    second = jnp.where(core == 0, other, half)
    return jnp.concatenate([first, second], axis=axis)


def add_over_heads(base, partial, core, starts):
    total = head_sum_half(partial, starts)
    mine = rows_from(base, starts[0], total.shape[0]).astype(f32)
    return both_halves((mine + total).astype(bf16), core)


def of_core(value, core):
    return lax.dynamic_index_in_dim(value, core, 1, keepdims=False)


def add_mixer(residual, arrived, own_weight, other_weight, core):
    peers, _, rows, channels = arrived.shape
    own = of_core(arrived, core).reshape(peers * rows, channels)
    other = of_core(arrived, 1 - core).reshape(peers * rows, channels)
    partial = jnp.dot(own, own_weight, preferred_element_type=f32)
    total = ring_sum(partial + jnp.dot(other, other_weight, preferred_element_type=f32))
    mine = of_core(residual.reshape(peers, 2, rows, -1), core).reshape(peers * rows, -1).astype(f32)
    half = (mine + total).astype(bf16).reshape(peers, 1, rows, -1)
    return both_halves(half, core, 1).reshape(residual.shape)


def exchange(value, axis):
    return lax.all_to_all(value, axis, 0, 0, tiled=True)


def to_everyone(value, axis):
    peers = lax.axis_size(axis)
    copies = jnp.broadcast_to(value[None], (peers, *value.shape))
    return exchange(copies, axis).reshape(peers * value.shape[0], *value.shape[1:])


def on_device(
    residual, lengths, ssm_state, tail_mix, tail_group, norm_first, mix_weight, group_weight, step_weight,
    conv_mix, conv_group, bias_mix, bias_group, step_bias, decay_log, skip_gain, gate_gain, out_weight,
    norm_second, up_weight, down_weight,
):
    peers = lax.axis_size(REQ)
    rows_dev = ssm_state.shape[0]
    rows, width_dev = residual.shape
    width_all = width_dev * peers
    mix_flat = mix_weight.reshape(width_dev, -1)
    pieces = input_projection(residual, norm_first[None], mix_flat, group_weight, step_weight.T)
    other_weight = swap_core(out_weight)
    arrived = exchange(pieces.reshape(peers, rows_dev, -1), REQ)
    copies, tail_mix_out, tail_group_out, u, decay, b = mixer_step(
        arrived, lengths, tail_mix, tail_group, conv_mix, conv_group, bias_mix, bias_group, step_bias,
        decay_log, skip_gain, gate_gain, ssm_state, width_all,
    )
    every_y = exchange(copies.reshape(2 * peers, rows_dev // 2, -1), REQ + ("c",))
    state_out = state_update(ssm_state, u, decay, b)
    core = lax.axis_index("c")
    place = core.astype(jnp.uint32)
    starts = (place * jnp.uint32(rows // 2), (jnp.uint32(1) - place) * jnp.uint32(rows // 2))
    every_y, state_out, core, starts = lax.optimization_barrier((every_y, state_out, core, starts))
    every_y = every_y.reshape(peers, 2, rows_dev // 2, -1)
    middle = add_mixer(residual, every_y, out_weight, other_weight, core)
    wide = middle.astype(f32)
    scaled_two = (wide * norm_second).astype(bf16)
    activation = jnp.dot(scaled_two, up_weight, preferred_element_type=f32).astype(bf16)
    hidden_dev = up_weight.shape[1]
    total = jnp.sum(wide * wide, axis=1, keepdims=True)
    high = lax.reduce_precision(total, 8, 7)
    mid = lax.reduce_precision(total - high, 8, 7)
    low = total - high - mid
    lane = lax.broadcasted_iota(jnp.int32, (rows, LANES), 1)
    columns = jnp.where(lane == 0, high, jnp.where(lane == 1, mid, jnp.where(lane == 2, low, 0.0))).astype(bf16)
    sent = jnp.concatenate([activation, columns], axis=1).reshape(peers, rows_dev, hidden_dev + LANES)
    sums = exchange(sent, REQ).astype(f32).sum(axis=0)
    squares = sums[:, hidden_dev : hidden_dev + 1] + sums[:, hidden_dev + 1 : hidden_dev + 2] + sums[:, hidden_dev + 2 : hidden_dev + 3]
    inverse = lax.rsqrt(squares / width_all + eps)
    hidden = jnp.square(jax.nn.relu(sums[:, :hidden_dev] * inverse)).astype(bf16)
    every_hidden = to_everyone(hidden, REQ)
    projected = jnp.dot(every_hidden, down_weight, preferred_element_type=f32)
    residual_out = add_over_heads(middle, projected, core, starts)
    return residual_out, state_out, jnp.transpose(tail_mix_out, (1, 0, 2)), tail_group_out


def solution(mesh):
    devices = mesh.devices
    finer = Mesh(devices.reshape(4, devices.shape[0] // 4, devices.shape[1] // 2, 2), REQ + HEAD)
    placed = (
        P(None, REQ),
        P(REQ),
        P(REQ, HEAD, None, None),
        P(REQ, None, HEAD),
        P(REQ, None, None, HEAD),
        P(REQ),
        P(REQ, None, HEAD),
        P(REQ, None, HEAD),
        P(REQ, HEAD),
        P(None, HEAD),
        P(None, None, HEAD),
        P(HEAD),
        P(None, HEAD),
        P(HEAD),
        P(HEAD),
        P(HEAD),
        P(HEAD),
        P(HEAD, REQ),
        P(REQ),
        P(REQ, HEAD),
        P(HEAD, REQ),
    )
    return jax.shard_map(
        on_device,
        mesh=finer,
        in_specs=placed,
        out_specs=(P(None, REQ), P(REQ, HEAD, None, None), P(REQ, None, HEAD), P(REQ, None, None, HEAD)),
        check_vma=False,
    )
```
